256 devices in a mesh: row: 16 (over x, y), col: 16 (over z, core).
Axes of the slice: x: 4, y: 4, z: 8, core: 2. Of those that a mesh axis runs over, the one named last changes fastest.
Arguments:
- root_block: bfloat16 [16, 256, 4096], P('row', None, 'col'), may hold values from -1 to 3, as said below
- l_one: bfloat16 [16, 256, 4096], P('row', None, 'col'), may hold values from -0.09375 to 0.09375
- dinv_one: bfloat16 [16, 128, 4096], P('row', None, 'col'), may hold values from -1 to 3, as said below
- l_two: bfloat16 [16, 384, 4096], P('row', None, 'col'), may hold values from -0.078125 to 0.078125
- dinv_two: bfloat16 [16, 64, 4096], P('row', None, 'col'), may hold values from -1 to 3, as said below
- l_three: bfloat16 [16, 448, 4096], P('row', None, 'col'), may hold values from -0.0625 to 0.0625
- dinv_three: bfloat16 [16, 32, 4096], P('row', None, 'col'), may hold values from -1 to 3, as said below
Outputs:
- sigma_one: float32 [16, 384, 4096], P('row', None, 'col')
- sigma_two: float32 [16, 448, 4096], P('row', None, 'col')
- sigma_three: float32 [16, 480, 4096], P('row', None, 'col')
The draws below stay inside these ranges and needn't reach their ends.
Inputs may be any that keep to these rules, and one draw needn't show every extreme that they name: Each node's diagonal block of root_block (in natural row order, in the node's columns) is exactly symmetric. `dinv_one`: each node's 2048 x 2048 block in natural row order is exactly symmetric. `dinv_two`: each node's 1024 x 1024 block in natural row order is exactly symmetric. `dinv_three`: each node's 512 x 512 block in natural row order is exactly symmetric.
All inputs are finite; a program needn't handle non-finite values.
Results may differ from the reference program's by a relative error of at most 0.0003.
Values may be sent and summed in bfloat16 or wider, within the bound.
A program may use at most 64 MiB of HBM per device.

```python
import jax
import jax.numpy as jnp
from jax import lax

S0 = 4096
S1 = 2048
S2 = 1024
S3 = 512
RUNS = 16


def arrange_blocks(raw_values, diagonal, block_width, node_count):
    scale_factor = 0.4 / jnp.sqrt(2.0 * block_width)
    identity = jnp.eye(block_width, dtype=jnp.float32)
    mixed = (raw_values + jnp.swapaxes(raw_values, 1, 2)) * scale_factor
    blocks = mixed * (1.0 - identity)[None] + identity[None] * diagonal[:, None, :]
    laid_out = jnp.transpose(blocks, (1, 0, 2)).reshape(block_width, node_count * block_width)
    return laid_out.reshape(RUNS, block_width // RUNS, node_count * block_width).astype(jnp.bfloat16)


def symmetric_normal(key, block_width, node_count):
    first_key = jax.random.fold_in(key, 11)
    second_key = jax.random.fold_in(key, 12)
    raw_values = jax.random.normal(first_key, (node_count, block_width, block_width), jnp.float32)
    diagonal = jax.random.uniform(second_key, (node_count, block_width), jnp.float32, 1.0, 2.0)
    return arrange_blocks(raw_values, diagonal, block_width, node_count)


def draw_root_block(key, part):
    return symmetric_normal(key, S0, 1)


def draw_dinv_one(key, part):
    return symmetric_normal(key, S1, 2)


def draw_dinv_two(key, part):
    return symmetric_normal(key, S2, 4)


def draw_dinv_three(key, part):
    return symmetric_normal(key, S3, 8)


def levels(stream_key, dims, split, least, top_value):
    factor_of, own = 1.0, jax.random.fold_in(stream_key, 6)
    for axis_at, shards_of in split:
        draws = jnp.exp(jax.random.uniform(jax.random.fold_in(own, axis_at), (shards_of,), jnp.float32, least / len(split), top_value / len(split)))
        factor_of = factor_of * jnp.repeat(draws, dims[axis_at] // shards_of).reshape([-1 if axis == axis_at else 1 for axis in range(len(dims))])
    return factor_of


def noise(own_key, extent, spread, bound, split=(), kind=jnp.bfloat16):
    level = levels(own_key, extent, split, -0.22, 0.18) if split else 1.0
    values = jax.random.normal(own_key, extent, jnp.float32) * spread * level
    return jnp.minimum(jnp.maximum(values, -bound), bound).astype(kind)


def setup_inputs(seed: int = 0) -> dict:
    seeds = jax.random.split(jax.random.key(seed), 8)
    return {
        "root_block": draw_root_block(jax.random.fold_in(seeds[7], 71), 0),
        "l_one": noise(seeds[1], (RUNS, S0 // RUNS, S0), S0 ** -0.5, 0.09375, ((0, 16), (2, 16))),
        "dinv_one": draw_dinv_one(jax.random.fold_in(seeds[7], 71), 0),
        "l_two": noise(seeds[3], (RUNS, (S0 + S1) // RUNS, S0), (S0 + S1) ** -0.5, 0.078125, ((0, 16), (2, 16))),
        "dinv_two": draw_dinv_two(jax.random.fold_in(seeds[7], 71), 0),
        "l_three": noise(seeds[5], (RUNS, (S0 + S1 + S2) // RUNS, S0), (S0 + S1 + S2) ** -0.5, 0.0625, ((0, 16), (2, 16))),
        "dinv_three": draw_dinv_three(jax.random.fold_in(seeds[7], 71), 0),
    }


exact_mode = lax.Precision.HIGHEST


def natural_rows(stored, block_widths):
    run_count = stored.shape[0]
    pieces = []
    row_start = 0
    for block_width in block_widths:
        row_count = block_width // run_count
        pieces.append(stored[:, row_start:row_start + row_count, :].reshape(block_width, stored.shape[2]))
        row_start = row_start + row_count
    return jnp.concatenate(pieces, 0)


def stored_rows(matrix, block_widths, run_count):
    pieces = []
    row_start = 0
    for block_width in block_widths:
        pieces.append(matrix[row_start:row_start + block_width].reshape(run_count, block_width // run_count, matrix.shape[1]))
        row_start = row_start + block_width
    return jnp.concatenate(pieces, 1)


def path_matrix(sigmas, block_widths, tree_level, node_index):
    bounds = [sum(block_widths[:block_index]) for block_index in range(tree_level + 1)]
    grid_rows = []
    for row_block in range(tree_level):
        row_parts = []
        for col_block in range(tree_level):
            if row_block <= col_block:
                ancestor = (node_index // 2 ** (tree_level - col_block)) * block_widths[col_block]
                block_part = sigmas[col_block][bounds[row_block]:bounds[row_block + 1], ancestor:ancestor + block_widths[col_block]]
                if row_block == col_block:
                    block_part = 0.5 * (block_part + block_part.T)
            else:
                ancestor = (node_index // 2 ** (tree_level - row_block)) * block_widths[row_block]
                block_part = sigmas[row_block][bounds[col_block]:bounds[col_block + 1], ancestor:ancestor + block_widths[row_block]].T
            row_parts.append(block_part)
        grid_rows.append(jnp.concatenate(row_parts, 1))
    return jnp.concatenate(grid_rows, 0)


def reference(root_block, l_one, dinv_one, l_two, dinv_two, l_three, dinv_three):
    block_widths = [S0, S1, S2, S3]
    sigmas = [natural_rows(root_block, [S0]).astype(jnp.float32)]
    factors = [l_one, l_two, l_three]
    inverses = [dinv_one, dinv_two, dinv_three]
    results = []
    for tree_level in range(1, 4):
        factor_matrix = natural_rows(factors[tree_level - 1], block_widths[:tree_level]).astype(jnp.float32)
        inverse_matrix = natural_rows(inverses[tree_level - 1], [block_widths[tree_level]]).astype(jnp.float32)
        node_width = block_widths[tree_level]
        columns = []
        for node_index in range(2 ** tree_level):
            first_col = node_index * node_width
            factor_cols = factor_matrix[:, first_col:first_col + node_width]
            path_block = path_matrix(sigmas, block_widths, tree_level, node_index)
            panel_part = -jnp.dot(path_block, factor_cols, precision=exact_mode, preferred_element_type=jnp.float32)
            inner_term = jnp.dot(panel_part.T, factor_cols, precision=exact_mode, preferred_element_type=jnp.float32)
            diag_part = inverse_matrix[:, first_col:first_col + node_width] - inner_term
            columns.append(jnp.concatenate([panel_part, diag_part], 0))
        sigma_level = jnp.concatenate(columns, 1)
        sigmas.append(sigma_level)
        results.append(stored_rows(sigma_level, block_widths[:tree_level + 1], RUNS))
    return results[0], results[1], results[2]
```

```python
import jax
import jax.numpy as jnp
from jax import lax
from jax.experimental import pallas as pl
from jax.experimental.pallas import tpu as pltpu
from jax.sharding import PartitionSpec as P

MESH = pl.DeviceIdType.MESH
F32 = jnp.float32
BF16 = jnp.bfloat16


def wrap(value, extent):
    return lax.rem(value + extent, extent)


def remote(src, dst, send_sem, recv_sem, device):
    return pltpu.make_async_remote_copy(
        src_ref=src, dst_ref=dst, send_sem=send_sem, recv_sem=recv_sem,
        device_id=device, device_id_type=MESH,
    )


def halves(value):
    high = value.astype(BF16)
    low = (value - high.astype(F32)).astype(BF16)
    return high, low


def product(left_tiles, right_tiles):
    left = jnp.concatenate(left_tiles, 1) if len(left_tiles) > 1 else left_tiles[0]
    right = jnp.concatenate(right_tiles, 0) if len(right_tiles) > 1 else right_tiles[0]
    return jnp.dot(left, right, preferred_element_type=F32)


def folded(value):
    rows = value.shape[0] // 2
    return value[:rows] + value[rows:]


class Plane:
    def __init__(self, source, held, send, recv, local, at):
        self.source, self.held, self.send, self.recv, self.local = source, held, send, recv, local
        self.x, self.y, self.c = at
        self.rows = source.shape[0]
        self.half = self.rows // 2
        self.quarter = self.half // 2
        self.started = []

    def device(self, x, y):
        return (wrap(x, 4) * 4 + wrap(y, 4), self.c)

    def targets(self, first):
        x, y = self.x, self.y
        along_x = [self.device(x + 1, y), self.device(x - 1, y)]
        along_y = [self.device(x, y + 1), self.device(x, y - 1)]
        return along_x + along_y if first else along_y + along_x

    def go(self, stage, lane, src, dst, device):
        copy = remote(src, dst, self.send.at[stage, lane], self.recv.at[stage, lane], device)
        copy.start()
        self.started.append(copy)

    def arrive(self, stage, lane, dst):
        remote(dst, dst, self.send.at[stage, lane], self.recv.at[stage, lane], self.device(self.x, self.y + 1)).wait_recv()

    def near(self, lane):
        x, y, held, half, rows = self.x, self.y, self.held, self.half, self.rows
        return [
            held.at[wrap(x - 1, 4), y, 0:half],
            held.at[wrap(x + 1, 4), y, 0:half],
            held.at[x, wrap(y - 1, 4), half:rows],
            held.at[x, wrap(y + 1, 4), half:rows],
        ][lane]

    def open(self):
        self.own = pltpu.make_async_copy(self.source, self.held.at[self.x, self.y], self.local)
        for lane, device in enumerate(self.targets(True)):
            part = slice(0, self.half) if lane < 2 else slice(self.half, self.rows)
            self.go(0, lane, self.source.at[part], self.held.at[self.x, self.y, part], device)
        self.own.start()

    def cross(self):
        x, y, held, half, quarter, rows = self.x, self.y, self.held, self.half, self.quarter, self.rows
        parts = [
            held.at[wrap(x - 1, 4), y, 0:quarter],
            held.at[wrap(x + 1, 4), y, quarter:half],
            held.at[x, wrap(y - 1, 4), half:half + quarter],
            held.at[x, wrap(y + 1, 4), half + quarter:rows],
        ]
        for lane, device in enumerate(self.targets(True)):
            self.arrive(0, lane, self.near(lane))
            self.go(1, lane, parts[lane], parts[lane], device)

    def spread(self):
        x, y, held, half, quarter, rows = self.x, self.y, self.held, self.half, self.quarter, self.rows
        far_x, far_y = wrap(x + 2, 4), wrap(y + 2, 4)
        for lane, part in enumerate([
            held.at[far_x, y, 0:quarter],
            held.at[far_x, y, quarter:half],
            held.at[x, far_y, half:half + quarter],
            held.at[x, far_y, half + quarter:rows],
        ]):
            self.arrive(1, lane, part)
        self.own.wait()
        line_x, line_y = held.at[:, y, 0:half], held.at[x, :, half:rows]
        for lane, device in enumerate(self.targets(False)):
            part = line_x if lane < 2 else line_y
            self.go(2, lane, part, part, device)

    def close(self):
        x, y, held, half, rows = self.x, self.y, self.held, self.half, self.rows
        whole = [
            held.at[:, wrap(y - 1, 4), 0:half],
            held.at[:, wrap(y + 1, 4), 0:half],
            held.at[wrap(x - 1, 4), :, half:rows],
            held.at[wrap(x + 1, 4), :, half:rows],
        ]
        parts = [
            held.at[0:2, wrap(y - 1, 4), 0:half],
            held.at[2:4, wrap(y + 1, 4), 0:half],
            held.at[wrap(x - 1, 4), 0:2, half:rows],
            held.at[wrap(x + 1, 4), 2:4, half:rows],
        ]
        for lane, device in enumerate(self.targets(False)):
            self.arrive(2, lane, whole[lane])
            self.go(3, lane, parts[lane], parts[lane], device)

    def finish(self):
        x, y, held, half, rows = self.x, self.y, self.held, self.half, self.rows
        far_x, far_y = wrap(x + 2, 4), wrap(y + 2, 4)
        for lane, part in enumerate([
            held.at[0:2, far_y, 0:half],
            held.at[2:4, far_y, 0:half],
            held.at[far_x, 0:2, half:rows],
            held.at[far_x, 2:4, half:rows],
        ]):
            self.arrive(3, lane, part)

    def block(self, start, width, tile):
        per_tile = 256 // width
        found = []
        for piece in range(per_tile):
            run = tile * per_tile + piece
            found.append(self.held[run // 4, run % 4, start:start + width])
        return found


class Ring:
    def __init__(self, source, held, send, recv, partner_send, partner_recv, local, at):
        self.source, self.held, self.send, self.recv = source, held, send, recv
        self.partner_send, self.partner_recv, self.local = partner_send, partner_recv, local
        self.r, self.z, self.core = at
        self.started = []

    def slot(self, z, core):
        return self.held.at[wrap(z, 8) * 2 + core, 0:256]

    def device(self, z, core):
        return (self.r, wrap(z, 8) * 2 + core)

    def go(self, step, lane, src, dst):
        shift = 1 if lane == 0 else -1
        copy = remote(src, dst, self.send.at[step, lane], self.recv.at[step, lane], self.device(self.z + shift, self.core))
        copy.start()
        self.started.append(copy)

    def share(self, index, src, dst):
        copy = remote(src, dst, self.partner_send.at[index], self.partner_recv.at[index], self.device(self.z, 1 - self.core))
        copy.start()
        self.started.append(copy)

    def arrive(self, step, lane, dst):
        remote(dst, dst, self.send.at[step, lane], self.recv.at[step, lane], self.device(self.z + 1, self.core)).wait_recv()

    def open(self):
        own = self.slot(self.z, self.core)
        for lane in range(2):
            self.go(0, lane, self.source, own)
        self.share(0, self.source, own)
        self.own = pltpu.make_async_copy(self.source, own, self.local)
        self.own.start()

    def step(self, number):
        for lane in range(2):
            distance = -number if lane == 0 else number
            tile = self.slot(self.z + distance, self.core)
            self.arrive(number - 1, lane, tile)
            if number < 3:
                self.go(number, lane, tile, tile)
            else:
                part = self.held.at[wrap(self.z + distance, 8) * 2 + self.core, 128 * lane:128 * lane + 128]
                self.go(number, lane, part, part)
            self.share(2 * number - 1 + lane, tile, tile)

    def finish(self):
        far = wrap(self.z + 4, 8) * 2 + self.core
        for lane in range(2):
            self.arrive(3, lane, self.held.at[far, 128 * lane:128 * lane + 128])
        tile = self.slot(self.z + 4, self.core)
        self.share(7, tile, tile)
        other = 1 - self.core
        for index, distance in enumerate([0, -1, 1, -2, 2, -3, 3, 4]):
            tile = self.slot(self.z + distance, other)
            remote(tile, tile, self.partner_send.at[index], self.partner_recv.at[index], self.device(self.z, other)).wait_recv()
        self.own.wait()


class Node:
    def __init__(self, held, rows, chips, send, recv, partner_send, partner_recv, at):
        self.held, self.rows, self.chips = held, rows, chips
        self.send, self.recv, self.partner_send, self.partner_recv = send, recv, partner_send, partner_recv
        self.r, self.z, self.core = at
        self.first = self.z - lax.rem(self.z, chips)
        self.place = lax.rem(self.z, chips)
        self.started = []

    def slot(self, place, core):
        return self.held.at[place * 2 + core, self.rows]

    def share(self, index, tile):
        copy = remote(tile, tile, self.partner_send.at[index], self.partner_recv.at[index],
                      (self.r, self.z * 2 + 1 - self.core))
        copy.start()
        self.started.append(copy)

    def open(self):
        tile = self.slot(self.place, self.core)
        for hop in range(1, self.chips):
            target = wrap(self.place + hop, self.chips)
            copy = remote(tile, tile, self.send.at[hop], self.recv.at[hop], (self.r, (self.first + target) * 2 + self.core))
            copy.start()
            self.started.append(copy)
        self.share(0, tile)

    def relay(self):
        for hop in range(1, self.chips):
            tile = self.slot(wrap(self.place - hop, self.chips), self.core)
            remote(tile, tile, self.send.at[hop], self.recv.at[hop], (self.r, self.z * 2 + 1 - self.core)).wait_recv()
            self.share(hop, tile)

    def finish(self):
        other = 1 - self.core
        for hop in range(self.chips):
            tile = self.slot(wrap(self.place - hop, self.chips), other)
            remote(tile, tile, self.partner_send.at[hop], self.partner_recv.at[hop], (self.r, self.z * 2 + other)).wait_recv()


class Turn:
    def __init__(self, source, place, whole, send, recv, partner_send, partner_recv, local, at):
        self.source, self.place, self.whole = source, place, whole
        self.send, self.recv, self.partner_send, self.partner_recv, self.local = send, recv, partner_send, partner_recv, local
        self.r, self.c, self.core = at
        self.started = []

    def open(self):
        self.own = pltpu.make_async_copy(self.source.at[self.r], self.place(self.r, self.core), self.local)
        self.own.start()
        for hop in range(1, 16):
            target = wrap(self.r + hop, 16)
            copy = remote(self.source.at[target], self.place(self.r, self.core), self.send.at[hop], self.recv.at[hop], (target, self.c))
            copy.start()
            self.started.append(copy)

    def relay(self):
        for hop in range(1, 16):
            part = self.place(wrap(self.r - hop, 16), self.core)
            remote(part, part, self.send.at[hop], self.recv.at[hop], (wrap(self.r + 1, 16), self.c)).wait_recv()
        self.own.wait()
        part = self.whole(self.core)
        copy = remote(part, part, self.partner_send, self.partner_recv, (self.r, self.c + 1 - 2 * self.core))
        copy.start()
        self.started.append(copy)

    def finish(self):
        part = self.whole(1 - self.core)
        remote(part, part, self.partner_send, self.partner_recv, (self.r, self.c + 1 - 2 * self.core)).wait_recv()


def kernel(root, l_one, l_two, l_three, d_one, d_two, d_three, out_one, out_two, out_three,
           p_zero, p_one, p_two, p_three, g_one, g_two, g_three, turn_one, turn_two, turn_cross, sums, gained,
           plane_send, plane_recv, ring_send, ring_recv, ring_core_send, ring_core_recv,
           node_send, node_recv, node_core_send, node_core_recv,
           turn_send, turn_recv, turn_core_send, turn_core_recv, last_send, last_recv, local):
    r, c = lax.axis_index("row"), lax.axis_index("col")
    x, y = lax.div(r, 4), lax.rem(r, 4)
    z, core = lax.div(c, 2), lax.rem(c, 2)
    eighth, quarter = lax.rem(c, 8), lax.rem(c, 4)

    barrier = pltpu.get_barrier_semaphore()
    for hop in range(1, 16):
        pl.semaphore_signal(barrier, inc=1, device_id=(wrap(r + hop, 16), c), device_id_type=MESH)
    for hop in range(1, 8):
        pl.semaphore_signal(barrier, inc=1, device_id=(r, wrap(z + hop, 8) * 2 + core), device_id_type=MESH)
    pl.semaphore_signal(barrier, inc=1, device_id=(r, z * 2 + 1 - core), device_id_type=MESH)
    pl.semaphore_wait(barrier, 23)

    planes = [
        Plane(source, held, plane_send.at[level], plane_recv.at[level], local.at[level], (x, y, c))
        for level, (source, held) in enumerate([(l_one, g_one), (l_two, g_two), (l_three, g_three)])
    ]
    one, two, three = planes
    ring = Ring(root, p_zero, ring_send, ring_recv, ring_core_send, ring_core_recv, local.at[3], (r, z, core))

    def node(index, held, rows, chips):
        return Node(held, rows, chips, node_send.at[index], node_recv.at[index], node_core_send.at[index],
                    node_core_recv.at[index], (r, z, core))

    s01 = node(0, p_one, slice(0, 512), 4)
    s11 = node(1, p_one, slice(512, 768), 4)
    s02 = node(2, p_two, slice(0, 512), 2)
    s12 = node(3, p_two, slice(512, 768), 2)
    s22 = node(4, p_two, slice(768, 896), 2)

    def turn(index, source, place, whole):
        return Turn(source, place, whole, turn_send.at[index], turn_recv.at[index], turn_core_send.at[index],
                    turn_core_recv.at[index], local.at[4 + index], (r, c, core))

    def rows_at(start, size, which):
        return pl.ds(pl.multiple_of(start + size * which, size), size)

    t01 = turn(0, turn_one, lambda run, which: p_zero.at[run, rows_at(256, 128, which)],
               lambda which: p_zero.at[:, rows_at(256, 128, which)])
    t02 = turn(1, turn_two, lambda run, which: p_zero.at[run, rows_at(512, 64, which)],
               lambda which: p_zero.at[:, rows_at(512, 64, which)])
    t12 = turn(2, turn_cross,
               lambda run, which: p_one.at[lax.div(run, 2), rows_at(768, 64, which),
                                           pl.ds(pl.multiple_of(lax.rem(run, 2) * 128, 128), 128)],
               lambda which: p_one.at[:, rows_at(768, 64, which)])

    def store(held, index, start, value):
        rows = value.shape[0]
        high, low = halves(value)
        held[index, start:start + rows] = high
        held[index, start + rows:start + 2 * rows] = low

    def zero_part(plane, first, last):
        return product([p_zero[k, first:last] for k in range(16)],
                       [piece for k in range(16) for piece in plane.block(0, 256, k)])

    def one_part(plane, first, last):
        return product([p_one[k, first:last] for k in range(8)],
                       [piece for k in range(8) for piece in plane.block(256, 128, k)])

    def two_part(plane, first, last):
        return product([p_two[k, first:last] for k in range(4)],
                       [piece for k in range(4) for piece in plane.block(384, 64, k)])

    one.open()
    ring.open()
    two.open()
    one.cross()
    ring.step(1)
    one.spread()
    ring.step(2)
    two.cross()
    three.open()
    one.close()
    ring.step(3)
    two.spread()
    three.cross()
    one.finish()
    ring.finish()

    value = -zero_part(one, 0, 256)
    store(p_one, eighth, 0, value)
    s01.open()
    out_one[0, 0:256] = value

    two.close()
    three.spread()
    s01.relay()
    s01.finish()
    for k in range(8):
        tile = p_one[k, rows_at(0, 256, core)]
        turned = tile.T
        turn_one[2 * k] = turned[0:128]
        turn_one[2 * k + 1] = turned[128:256]
    t01.open()

    two.finish()
    value = -(zero_part(two, 0, 256) + folded(one_part(two, 0, 512)))
    store(p_two, quarter, 0, value)
    s02.open()
    out_two[0, 0:256] = value

    t01.relay()
    t01.finish()
    value = d_one[...].astype(F32) - folded(zero_part(one, 256, 512))
    store(p_one, eighth, 512, value)
    s11.open()
    out_one[0, 256:384] = value

    three.close()
    s02.relay()
    s02.finish()
    for k in range(4):
        tile = p_two[k, rows_at(0, 256, core)]
        turned = tile.T
        for piece in range(4):
            turn_two[4 * k + piece] = turned[64 * piece:64 * piece + 64]
    t02.open()

    s11.relay()
    s11.finish()
    value = -folded(zero_part(two, 256, 512) + one_part(two, 512, 768))
    store(p_two, quarter, 512, value)
    s12.open()
    out_two[0, 256:384] = value

    s12.relay()
    s12.finish()
    for k in range(4):
        tile = p_two[k, rows_at(512, 128, core)]
        turned = tile.T
        for piece in range(4):
            turn_cross[4 * k + piece] = turned[64 * piece:64 * piece + 64]
    t12.open()

    three.finish()
    upper = -(zero_part(three, 0, 256) + folded(one_part(three, 0, 512)) + folded(two_part(three, 0, 512)))
    out_three[0, 0:256] = upper
    high, low = halves(upper)
    p_three[core, 0:256] = high
    p_three[core, 448:704] = low
    middle = -folded(zero_part(three, 256, 512) + one_part(three, 512, 768) + two_part(three, 512, 768))
    out_three[0, 256:384] = middle
    high, low = halves(middle)
    p_three[core, 256:384] = high
    p_three[core, 704:832] = low

    t02.relay()
    t12.relay()
    t02.finish()
    t12.finish()
    value = d_two[...].astype(F32) - folded(zero_part(two, 512, 640) + one_part(two, 768, 896))
    store(p_two, quarter, 768, value)
    s22.open()
    out_two[0, 384:448] = value
    s22.relay()
    s22.finish()

    lower = -folded(zero_part(three, 512, 640) + one_part(three, 768, 896) + two_part(three, 768, 896))
    out_three[0, 384:448] = lower
    high, low = halves(lower)
    p_three[core, 384:448] = high
    p_three[core, 832:896] = low
    mine = p_three.at[core]
    swap = remote(mine, mine, last_send.at[0], last_recv.at[0], (r, z * 2 + 1 - core))
    swap.start()
    theirs = p_three.at[1 - core]
    remote(theirs, theirs, last_send.at[0], last_recv.at[0], (r, z * 2 + 1 - core)).wait_recv()
    factor = l_three[...]
    for which in range(2):
        turned = jnp.concatenate([p_three[which, 0:448].T, p_three[which, 448:896].T], 0)
        partial = folded(jnp.dot(turned, factor, preferred_element_type=F32))
        for piece in range(8):
            sums[8 * which + piece] = partial[32 * piece:32 * piece + 32]
    final = []
    for hop in range(1, 16):
        target = wrap(r + hop, 16)
        copy = remote(sums.at[target], gained.at[r], last_send.at[hop], last_recv.at[hop], (target, c))
        copy.start()
        final.append(copy)
    total = sums[r]
    for hop in range(1, 16):
        source = wrap(r - hop, 16)
        part = gained.at[source]
        remote(part, part, last_send.at[hop], last_recv.at[hop], (wrap(r + 1, 16), c)).wait_recv()
        total = total + gained[source]
    out_three[0, 448:480] = d_three[...].astype(F32) - total

    swap.wait_send()
    for group in [one, two, three, ring, s01, s11, s02, s12, s22, t01, t02, t12]:
        for copy in group.started:
            copy.wait_send()
    for copy in final:
        copy.wait_send()


def per_device(root_block, l_one, dinv_one, l_two, dinv_two, l_three, dinv_three):
    vmem = pl.BlockSpec(memory_space=pltpu.VMEM)
    dma = pltpu.SemaphoreType.DMA
    return pl.pallas_call(
        kernel,
        out_shape=(
            jax.ShapeDtypeStruct((1, 384, 256), F32),
            jax.ShapeDtypeStruct((1, 448, 256), F32),
            jax.ShapeDtypeStruct((1, 480, 256), F32),
        ),
        in_specs=[vmem] * 7,
        out_specs=(vmem, vmem, vmem),
        scratch_shapes=[
            pltpu.VMEM((16, 640, 256), BF16),
            pltpu.VMEM((8, 896, 256), BF16),
            pltpu.VMEM((4, 896, 256), BF16),
            pltpu.VMEM((2, 896, 256), BF16),
            pltpu.VMEM((4, 4, 256, 256), BF16),
            pltpu.VMEM((4, 4, 384, 256), BF16),
            pltpu.VMEM((4, 4, 448, 256), BF16),
            pltpu.VMEM((16, 128, 256), BF16),
            pltpu.VMEM((16, 64, 256), BF16),
            pltpu.VMEM((16, 64, 128), BF16),
            pltpu.VMEM((16, 32, 256), F32),
            pltpu.VMEM((16, 32, 256), F32),
            dma((3, 4, 4)), dma((3, 4, 4)),
            dma((4, 2)), dma((4, 2)), dma((8,)), dma((8,)),
            dma((5, 4)), dma((5, 4)), dma((5, 4)), dma((5, 4)),
            dma((3, 16)), dma((3, 16)), dma((3,)), dma((3,)),
            dma((16,)), dma((16,)),
            dma((7,)),
        ],
        compiler_params=pltpu.CompilerParams(
            collective_id=0, has_side_effects=True, vmem_limit_bytes=60 * 1024 * 1024
        ),
    )(root_block[0], l_one[0], l_two[0], l_three[0], dinv_one[0], dinv_two[0], dinv_three[0])


def solution(mesh):
    placed = (P("row", None, "col"),) * 7
    return jax.shard_map(
        per_device,
        mesh=mesh,
        in_specs=placed,
        out_specs=(P("row", None, "col"), P("row", None, "col"), P("row", None, "col")),
        check_vma=False,
    )
```

```python
import jax
import jax.numpy as jnp
from jax import lax
from jax.experimental import pallas as pl
from jax.experimental.pallas import tpu as pltpu
from jax.sharding import PartitionSpec as P

MESH = pl.DeviceIdType.MESH
F32 = jnp.float32
BF16 = jnp.bfloat16


def wrap(value, extent):
    return lax.rem(value + extent, extent)


def remote(src, dst, send_sem, recv_sem, device):
    return pltpu.make_async_remote_copy(
        src_ref=src, dst_ref=dst, send_sem=send_sem, recv_sem=recv_sem,
        device_id=device, device_id_type=MESH,
    )


def halves(value):
    high = value.astype(BF16)
    low = (value - high.astype(F32)).astype(BF16)
    return high, low


def product(left_tiles, right_tiles):
    left = jnp.concatenate(left_tiles, 1) if len(left_tiles) > 1 else left_tiles[0]
    right = jnp.concatenate(right_tiles, 0) if len(right_tiles) > 1 else right_tiles[0]
    return jnp.dot(left, right, preferred_element_type=F32)


def folded(value):
    rows = value.shape[0] // 2
    return value[:rows] + value[rows:]


def folded_halves(value):
    rows = value.shape[0] // 2
    return jnp.concatenate([folded(value[:rows]), folded(value[rows:])], 0)


class Plane:
    def __init__(self, source, held, send, recv, local, at):
        self.source, self.held, self.send, self.recv, self.local = source, held, send, recv, local
        self.x, self.y, self.c = at
        self.rows = source.shape[0]
        self.half = self.rows // 2
        self.quarter = self.half // 2
        self.started = []

    def device(self, x, y):
        return (wrap(x, 4) * 4 + wrap(y, 4), self.c)

    def targets(self, first):
        x, y = self.x, self.y
        along_x = [self.device(x + 1, y), self.device(x - 1, y)]
        along_y = [self.device(x, y + 1), self.device(x, y - 1)]
        return along_x + along_y if first else along_y + along_x

    def go(self, stage, lane, src, dst, device):
        copy = remote(src, dst, self.send.at[stage, lane], self.recv.at[stage, lane], device)
        copy.start()
        self.started.append(copy)

    def arrive(self, stage, lane, dst):
        remote(dst, dst, self.send.at[stage, lane], self.recv.at[stage, lane], self.device(self.x, self.y + 1)).wait_recv()

    def near(self, lane):
        x, y, held, half, rows = self.x, self.y, self.held, self.half, self.rows
        return [
            held.at[wrap(x - 1, 4), y, 0:half],
            held.at[wrap(x + 1, 4), y, 0:half],
            held.at[x, wrap(y - 1, 4), half:rows],
            held.at[x, wrap(y + 1, 4), half:rows],
        ][lane]

    def open(self):
        self.own = pltpu.make_async_copy(self.source, self.held.at[self.x, self.y], self.local)
        for lane, device in enumerate(self.targets(True)):
            part = slice(0, self.half) if lane < 2 else slice(self.half, self.rows)
            self.go(0, lane, self.source.at[part], self.held.at[self.x, self.y, part], device)
        self.own.start()

    def cross(self):
        x, y, held, half, quarter, rows = self.x, self.y, self.held, self.half, self.quarter, self.rows
        parts = [
            held.at[wrap(x - 1, 4), y, 0:quarter],
            held.at[wrap(x + 1, 4), y, quarter:half],
            held.at[x, wrap(y - 1, 4), half:half + quarter],
            held.at[x, wrap(y + 1, 4), half + quarter:rows],
        ]
        for lane, device in enumerate(self.targets(True)):
            self.arrive(0, lane, self.near(lane))
            self.go(1, lane, parts[lane], parts[lane], device)

    def spread(self):
        x, y, held, half, quarter, rows = self.x, self.y, self.held, self.half, self.quarter, self.rows
        far_x, far_y = wrap(x + 2, 4), wrap(y + 2, 4)
        for lane, part in enumerate([
            held.at[far_x, y, 0:quarter],
            held.at[far_x, y, quarter:half],
            held.at[x, far_y, half:half + quarter],
            held.at[x, far_y, half + quarter:rows],
        ]):
            self.arrive(1, lane, part)
        self.own.wait()
        line_x, line_y = held.at[:, y, 0:half], held.at[x, :, half:rows]
        for lane, device in enumerate(self.targets(False)):
            part = line_x if lane < 2 else line_y
            self.go(2, lane, part, part, device)

    def close(self):
        x, y, held, half, rows = self.x, self.y, self.held, self.half, self.rows
        whole = [
            held.at[:, wrap(y - 1, 4), 0:half],
            held.at[:, wrap(y + 1, 4), 0:half],
            held.at[wrap(x - 1, 4), :, half:rows],
            held.at[wrap(x + 1, 4), :, half:rows],
        ]
        parts = [
            held.at[0:2, wrap(y - 1, 4), 0:half],
            held.at[2:4, wrap(y + 1, 4), 0:half],
            held.at[wrap(x - 1, 4), 0:2, half:rows],
            held.at[wrap(x + 1, 4), 2:4, half:rows],
        ]
        for lane, device in enumerate(self.targets(False)):
            self.arrive(2, lane, whole[lane])
            self.go(3, lane, parts[lane], parts[lane], device)

    def finish(self):
        x, y, held, half, rows = self.x, self.y, self.held, self.half, self.rows
        far_x, far_y = wrap(x + 2, 4), wrap(y + 2, 4)
        for lane, part in enumerate([
            held.at[0:2, far_y, 0:half],
            held.at[2:4, far_y, 0:half],
            held.at[far_x, 0:2, half:rows],
            held.at[far_x, 2:4, half:rows],
        ]):
            self.arrive(3, lane, part)

    def block(self, start, width, tile):
        per_tile = 256 // width
        found = []
        for piece in range(per_tile):
            run = tile * per_tile + piece
            found.append(self.held[run // 4, run % 4, start:start + width])
        return found


class Ring:
    def __init__(self, source, held, send, recv, partner_send, partner_recv, local, at):
        self.source, self.held, self.send, self.recv = source, held, send, recv
        self.partner_send, self.partner_recv, self.local = partner_send, partner_recv, local
        self.r, self.z, self.core = at
        self.started = []

    def slot(self, z, core):
        return self.held.at[wrap(z, 8) * 2 + core, 0:256]

    def device(self, z, core):
        return (self.r, wrap(z, 8) * 2 + core)

    def go(self, step, lane, src, dst):
        shift = 1 if lane == 0 else -1
        copy = remote(src, dst, self.send.at[step, lane], self.recv.at[step, lane], self.device(self.z + shift, self.core))
        copy.start()
        self.started.append(copy)

    def share(self, index, src, dst):
        copy = remote(src, dst, self.partner_send.at[index], self.partner_recv.at[index], self.device(self.z, 1 - self.core))
        copy.start()
        self.started.append(copy)

    def arrive(self, step, lane, dst):
        remote(dst, dst, self.send.at[step, lane], self.recv.at[step, lane], self.device(self.z + 1, self.core)).wait_recv()

    def open(self):
        own = self.slot(self.z, self.core)
        for lane in range(2):
            self.go(0, lane, self.source, own)
        self.share(0, self.source, own)
        self.own = pltpu.make_async_copy(self.source, own, self.local)
        self.own.start()

    def step(self, number):
        for lane in range(2):
            distance = -number if lane == 0 else number
            tile = self.slot(self.z + distance, self.core)
            self.arrive(number - 1, lane, tile)
            if number < 3:
                self.go(number, lane, tile, tile)
            else:
                part = self.held.at[wrap(self.z + distance, 8) * 2 + self.core, 128 * lane:128 * lane + 128]
                self.go(number, lane, part, part)
            self.share(2 * number - 1 + lane, tile, tile)

    def finish(self):
        far = wrap(self.z + 4, 8) * 2 + self.core
        for lane in range(2):
            self.arrive(3, lane, self.held.at[far, 128 * lane:128 * lane + 128])
        tile = self.slot(self.z + 4, self.core)
        self.share(7, tile, tile)
        other = 1 - self.core
        for index, distance in enumerate([0, -1, 1, -2, 2, -3, 3, 4]):
            tile = self.slot(self.z + distance, other)
            remote(tile, tile, self.partner_send.at[index], self.partner_recv.at[index], self.device(self.z, other)).wait_recv()
        self.own.wait()


class Node:
    def __init__(self, held, rows, chips, send, recv, partner_send, partner_recv, at):
        self.held, self.rows, self.chips = held, rows, chips
        self.send, self.recv, self.partner_send, self.partner_recv = send, recv, partner_send, partner_recv
        self.r, self.z, self.core = at
        self.first = self.z - lax.rem(self.z, chips)
        self.place = lax.rem(self.z, chips)
        self.started = []

    def slot(self, place, core):
        return self.held.at[place * 2 + core, self.rows]

    def share(self, index, tile):
        copy = remote(tile, tile, self.partner_send.at[index], self.partner_recv.at[index],
                      (self.r, self.z * 2 + 1 - self.core))
        copy.start()
        self.started.append(copy)

    def open(self):
        tile = self.slot(self.place, self.core)
        for hop in range(1, self.chips):
            target = wrap(self.place + hop, self.chips)
            copy = remote(tile, tile, self.send.at[hop], self.recv.at[hop], (self.r, (self.first + target) * 2 + self.core))
            copy.start()
            self.started.append(copy)
        self.share(0, tile)

    def relay(self):
        for hop in range(1, self.chips):
            tile = self.slot(wrap(self.place - hop, self.chips), self.core)
            remote(tile, tile, self.send.at[hop], self.recv.at[hop], (self.r, self.z * 2 + 1 - self.core)).wait_recv()
            self.share(hop, tile)

    def finish(self):
        other = 1 - self.core
        for hop in range(self.chips):
            tile = self.slot(wrap(self.place - hop, self.chips), other)
            remote(tile, tile, self.partner_send.at[hop], self.partner_recv.at[hop], (self.r, self.z * 2 + other)).wait_recv()


class Chain:
    def __init__(self, held, rows, send, recv, partner_send, partner_recv, at):
        self.held, self.rows = held, rows
        self.send, self.recv, self.partner_send, self.partner_recv = send, recv, partner_send, partner_recv
        self.r, self.z, self.core = at
        self.first = self.z - lax.rem(self.z, 4)
        place = lax.rem(self.z, 4)
        upper, odd = lax.div(place, 2), lax.rem(place, 2)
        self.beside, self.across = place + 1 - 2 * odd, 3 - place
        self.inner = (upper + odd) == 1
        self.order = [place, self.beside, 2 - upper, 3 - 3 * upper]
        self.started, self.started_inner = [], []

    def slot(self, place, core):
        return self.held.at[place * 2 + core, self.rows]

    def copy(self, index, lane, place, target):
        tile = self.slot(place, self.core)
        return remote(tile, tile, self.send.at[index], self.recv.at[lane], (self.r, (self.first + target) * 2 + self.core))

    def share(self, index):
        tile = self.slot(self.order[index], self.core)
        copy = remote(tile, tile, self.partner_send.at[index], self.partner_recv.at[index],
                      (self.r, self.z * 2 + 1 - self.core))
        copy.start()
        self.started.append(copy)

    def inward(self, copy):
        self.started_inner.append(copy)

        @pl.when(self.inner)
        def _():
            copy.start()

    def open(self):
        self.inward(self.copy(1, 1, self.order[0], self.across))
        copy = self.copy(0, 0, self.order[0], self.beside)
        copy.start()
        self.started.append(copy)
        self.share(0)

    def relay(self):
        targets = [self.across, self.beside, self.beside]
        lanes = [2, 1, 2]
        for lane in range(3):
            tile = self.slot(self.order[lane + 1], self.core)
            remote(tile, tile, self.send.at[0], self.recv.at[lane], (self.r, self.z * 2 + 1 - self.core)).wait_recv()
            self.inward(self.copy(2 + lane, lanes[lane], self.order[lane + 1], targets[lane]))
            self.share(lane + 1)

    def finish(self):
        other = 1 - self.core
        for index in range(4):
            tile = self.slot(self.order[index], other)
            remote(tile, tile, self.partner_send.at[index], self.partner_recv.at[index], (self.r, self.z * 2 + other)).wait_recv()

    def drain(self):
        @pl.when(self.inner)
        def _():
            for copy in self.started_inner:
                copy.wait_send()


class Turn:
    def __init__(self, source, place, whole, send, recv, partner_send, partner_recv, local, at):
        self.source, self.place, self.whole = source, place, whole
        self.send, self.recv, self.partner_send, self.partner_recv, self.local = send, recv, partner_send, partner_recv, local
        self.r, self.c, self.core = at
        self.started = []

    def open(self):
        self.own = pltpu.make_async_copy(self.source.at[self.r], self.place(self.r, self.core), self.local)
        self.own.start()
        for hop in range(1, 16):
            target = wrap(self.r + hop, 16)
            copy = remote(self.source.at[target], self.place(self.r, self.core), self.send.at[hop], self.recv.at[hop], (target, self.c))
            copy.start()
            self.started.append(copy)

    def relay(self):
        for hop in range(1, 16):
            part = self.place(wrap(self.r - hop, 16), self.core)
            remote(part, part, self.send.at[hop], self.recv.at[hop], (wrap(self.r + 1, 16), self.c)).wait_recv()
        self.own.wait()
        part = self.whole(self.core)
        copy = remote(part, part, self.partner_send, self.partner_recv, (self.r, self.c + 1 - 2 * self.core))
        copy.start()
        self.started.append(copy)

    def finish(self):
        part = self.whole(1 - self.core)
        remote(part, part, self.partner_send, self.partner_recv, (self.r, self.c + 1 - 2 * self.core)).wait_recv()


def kernel(root, l_one, l_two, l_three, d_one, d_two, d_three, out_one, out_two, out_three,
           p_zero, p_one, p_two, p_three, g_one, g_two, g_three, turn_one, turn_two, turn_cross, sums, gained,
           plane_send, plane_recv, ring_send, ring_recv, ring_core_send, ring_core_recv,
           node_send, node_recv, node_core_send, node_core_recv,
           chain_send, chain_recv, chain_core_send, chain_core_recv, swap_send, swap_recv,
           turn_send, turn_recv, turn_core_send, turn_core_recv, last_send, last_recv, local):
    r, c = lax.axis_index("row"), lax.axis_index("col")
    x, y = lax.div(r, 4), lax.rem(r, 4)
    z, core = lax.div(c, 2), lax.rem(c, 2)
    eighth, quarter = lax.rem(c, 8), lax.rem(c, 4)

    barrier = pltpu.get_barrier_semaphore()
    for hop in range(1, 16):
        pl.semaphore_signal(barrier, inc=1, device_id=(wrap(r + hop, 16), c), device_id_type=MESH)
    for hop in range(1, 8):
        pl.semaphore_signal(barrier, inc=1, device_id=(r, wrap(z + hop, 8) * 2 + core), device_id_type=MESH)
    pl.semaphore_signal(barrier, inc=1, device_id=(r, z * 2 + 1 - core), device_id_type=MESH)
    pl.semaphore_wait(barrier, 23)

    planes = [
        Plane(source, held, plane_send.at[level], plane_recv.at[level], local.at[level], (x, y, c))
        for level, (source, held) in enumerate([(l_one, g_one), (l_two, g_two), (l_three, g_three)])
    ]
    one, two, three = planes
    ring = Ring(root, p_zero, ring_send, ring_recv, ring_core_send, ring_core_recv, local.at[3], (r, z, core))

    def node(index, held, rows, chips):
        return Node(held, rows, chips, node_send.at[index], node_recv.at[index], node_core_send.at[index],
                    node_core_recv.at[index], (r, z, core))

    def chain(index, held, rows):
        return Chain(held, rows, chain_send.at[index], chain_recv.at[index], chain_core_send.at[index],
                     chain_core_recv.at[index], (r, z, core))

    s01 = [chain(0, p_one, slice(0, 256)), chain(1, p_one, slice(256, 512))]
    s11 = chain(2, p_one, slice(512, 768))
    s02 = node(0, p_two, slice(0, 512), 2)
    s12 = node(1, p_two, slice(512, 768), 2)
    s22 = node(2, p_two, slice(768, 896), 2)

    def turn(index, source, place, whole):
        return Turn(source, place, whole, turn_send.at[index], turn_recv.at[index], turn_core_send.at[index],
                    turn_core_recv.at[index], local.at[4 + index], (r, c, core))

    def rows_at(start, size, which):
        return pl.ds(pl.multiple_of(start + size * which, size), size)

    def half_turn(half):
        lanes = slice(128 * half, 128 * half + 128)
        return turn(2 + half, turn_one.at[half], lambda run, which: p_zero.at[run, rows_at(256, 128, which), lanes],
                    lambda which: p_zero.at[:, rows_at(256, 128, which), lanes])

    t01 = [half_turn(0), half_turn(1)]
    t02 = turn(0, turn_two, lambda run, which: p_zero.at[run, rows_at(512, 64, which)],
               lambda which: p_zero.at[:, rows_at(512, 64, which)])
    t12 = turn(1, turn_cross,
               lambda run, which: p_one.at[lax.div(run, 2), rows_at(768, 64, which),
                                           pl.ds(pl.multiple_of(lax.rem(run, 2) * 128, 128), 128)],
               lambda which: p_one.at[:, rows_at(768, 64, which)])

    def store(held, index, start, value):
        rows = value.shape[0]
        high, low = halves(value)
        held[index, start:start + rows] = high
        held[index, start + rows:start + 2 * rows] = low

    def zero_part(plane, first, last):
        return product([p_zero[k, first:last] for k in range(16)],
                       [piece for k in range(16) for piece in plane.block(0, 256, k)])

    def one_part(plane, first, last):
        return product([p_one[k, first:last] for k in range(8)],
                       [piece for k in range(8) for piece in plane.block(256, 128, k)])

    def two_part(plane, first, last):
        return product([p_two[k, first:last] for k in range(4)],
                       [piece for k in range(4) for piece in plane.block(384, 64, k)])

    one.open()
    ring.open()
    one.cross()
    ring.step(1)
    one.spread()
    two.open()
    ring.step(2)
    one.close()
    two.cross()
    three.open()
    ring.step(3)
    one.finish()
    two.spread()
    three.cross()
    ring.finish()

    for half in range(2):
        value = -zero_part(one, 128 * half, 128 * half + 128)
        store(p_one, eighth, 256 * half, value)
        s01[half].open()
        out_one[0, 128 * half:128 * half + 128] = value

    two.close()
    three.spread()
    for half in range(2):
        s01[half].relay()
        s01[half].finish()
        for k in range(8):
            tile = p_one[k, rows_at(256 * half, 128, core)]
            turned = tile.T
            turn_one[half, 2 * k] = turned[0:128]
            turn_one[half, 2 * k + 1] = turned[128:256]
        t01[half].open()

    two.finish()
    value = -(zero_part(two, 0, 256) + folded_halves(one_part(two, 0, 512)))
    store(p_two, quarter, 0, value)
    s02.open()
    out_two[0, 0:256] = value

    for half in range(2):
        t01[half].relay()
    for half in range(2):
        t01[half].finish()
    value = d_one[...].astype(F32) - folded(zero_part(one, 256, 512))
    store(p_one, eighth, 512, value)
    s11.open()
    out_one[0, 256:384] = value

    three.close()
    s02.relay()
    s02.finish()
    for k in range(4):
        tile = p_two[k, rows_at(0, 256, core)]
        turned = tile.T
        for piece in range(4):
            turn_two[4 * k + piece] = turned[64 * piece:64 * piece + 64]
    t02.open()

    s11.relay()
    s11.finish()
    value = -folded(zero_part(two, 256, 512) + one_part(two, 512, 768))
    store(p_two, quarter, 512, value)
    s12.open()
    out_two[0, 256:384] = value

    s12.relay()
    s12.finish()
    for k in range(4):
        tile = p_two[k, rows_at(512, 128, core)]
        turned = tile.T
        for piece in range(4):
            turn_cross[4 * k + piece] = turned[64 * piece:64 * piece + 64]
    t12.open()

    three.finish()
    upper = -(zero_part(three, 0, 256) + folded_halves(one_part(three, 0, 512)) + folded(two_part(three, 0, 512)))
    out_three[0, 0:256] = upper
    high, low = halves(upper)
    p_three[core, 0:256] = high
    p_three[core, 384:640] = low
    middle = -folded(zero_part(three, 256, 512) + one_part(three, 512, 768) + two_part(three, 512, 768))
    out_three[0, 256:384] = middle
    high, low = halves(middle)
    p_three[core, 256:384] = high
    p_three[core, 640:768] = low

    def swapped(index, rows):
        mine, theirs = p_three.at[core, rows], p_three.at[1 - core, rows]
        device = (r, z * 2 + 1 - core)
        return (remote(mine, mine, swap_send.at[index], swap_recv.at[index], device),
                remote(theirs, theirs, swap_send.at[index], swap_recv.at[index], device))

    def inner_terms(which, start, size, factor):
        turned = jnp.concatenate([p_three[which, start:start + size].T, p_three[which, start + size:start + 2 * size].T], 0)
        return folded(jnp.dot(turned, factor, preferred_element_type=F32))

    first_swap, first_gain = swapped(0, slice(0, 768))
    first_swap.start()

    t02.relay()
    t12.relay()
    t02.finish()
    t12.finish()
    value = d_two[...].astype(F32) - folded(zero_part(two, 512, 640) + one_part(two, 768, 896))
    store(p_two, quarter, 768, value)
    s22.open()
    out_two[0, 384:448] = value
    first_gain.wait_recv()
    for which in range(2):
        partial = inner_terms(which, 0, 384, l_three[0:384])
        for piece in range(8):
            sums[8 * which + piece] = partial[32 * piece:32 * piece + 32]
    s22.relay()
    s22.finish()

    lower = -folded(zero_part(three, 512, 640) + one_part(three, 768, 896) + two_part(three, 768, 896))
    high, low = halves(lower)
    p_three[core, 768:832] = high
    p_three[core, 832:896] = low
    last_swap, last_gain = swapped(1, slice(768, 896))
    last_swap.start()
    out_three[0, 384:448] = lower
    last_gain.wait_recv()
    for which in range(2):
        partial = inner_terms(which, 768, 64, l_three[384:448])
        for piece in range(8):
            sums[8 * which + piece] = sums[8 * which + piece] + partial[32 * piece:32 * piece + 32]
    final = []
    for hop in range(1, 16):
        target = wrap(r + hop, 16)
        copy = remote(sums.at[target], gained.at[r], last_send.at[hop], last_recv.at[hop], (target, c))
        copy.start()
        final.append(copy)
    total = sums[r]
    for hop in range(1, 16):
        source = wrap(r - hop, 16)
        part = gained.at[source]
        remote(part, part, last_send.at[hop], last_recv.at[hop], (wrap(r + 1, 16), c)).wait_recv()
        total = total + gained[source]
    out_three[0, 448:480] = d_three[...].astype(F32) - total

    first_swap.wait_send()
    last_swap.wait_send()
    for group in [one, two, three, ring, *s01, s11, s02, s12, s22, *t01, t02, t12]:
        for copy in group.started:
            copy.wait_send()
    for group in [*s01, s11]:
        group.drain()
    for copy in final:
        copy.wait_send()


def per_device(root_block, l_one, dinv_one, l_two, dinv_two, l_three, dinv_three):
    vmem = pl.BlockSpec(memory_space=pltpu.VMEM)
    dma = pltpu.SemaphoreType.DMA
    return pl.pallas_call(
        kernel,
        out_shape=(
            jax.ShapeDtypeStruct((1, 384, 256), F32),
            jax.ShapeDtypeStruct((1, 448, 256), F32),
            jax.ShapeDtypeStruct((1, 480, 256), F32),
        ),
        in_specs=[vmem] * 7,
        out_specs=(vmem, vmem, vmem),
        scratch_shapes=[
            pltpu.VMEM((16, 640, 256), BF16),
            pltpu.VMEM((8, 896, 256), BF16),
            pltpu.VMEM((4, 896, 256), BF16),
            pltpu.VMEM((2, 896, 256), BF16),
            pltpu.VMEM((4, 4, 256, 256), BF16),
            pltpu.VMEM((4, 4, 384, 256), BF16),
            pltpu.VMEM((4, 4, 448, 256), BF16),
            pltpu.VMEM((2, 16, 128, 128), BF16),
            pltpu.VMEM((16, 64, 256), BF16),
            pltpu.VMEM((16, 64, 128), BF16),
            pltpu.VMEM((16, 32, 256), F32),
            pltpu.VMEM((16, 32, 256), F32),
            dma((3, 4, 4)), dma((3, 4, 4)),
            dma((4, 2)), dma((4, 2)), dma((8,)), dma((8,)),
            dma((3, 2)), dma((3, 2)), dma((3, 2)), dma((3, 2)),
            dma((3, 5)), dma((3, 3)), dma((3, 4)), dma((3, 4)), dma((2,)), dma((2,)),
            dma((4, 16)), dma((4, 16)), dma((4,)), dma((4,)),
            dma((16,)), dma((16,)),
            dma((8,)),
        ],
        compiler_params=pltpu.CompilerParams(
            collective_id=0, has_side_effects=True, vmem_limit_bytes=60 * 1024 * 1024
        ),
    )(root_block[0], l_one[0], l_two[0], l_three[0], dinv_one[0], dinv_two[0], dinv_three[0])


def solution(mesh):
    placed = (P("row", None, "col"),) * 7
    return jax.shard_map(
        per_device,
        mesh=mesh,
        in_specs=placed,
        out_specs=(P("row", None, "col"), P("row", None, "col"), P("row", None, "col")),
        check_vma=False,
    )
```

```python
import jax
import jax.numpy as jnp
from jax import lax
from jax.experimental import pallas as pl
from jax.experimental.pallas import tpu as pltpu
from jax.sharding import PartitionSpec as P

MESH = pl.DeviceIdType.MESH
F32 = jnp.float32
BF16 = jnp.bfloat16


def wrap(value, extent):
    return lax.rem(value + extent, extent)


def remote(src, dst, send_sem, recv_sem, device):
    return pltpu.make_async_remote_copy(
        src_ref=src, dst_ref=dst, send_sem=send_sem, recv_sem=recv_sem,
        device_id=device, device_id_type=MESH,
    )


def halves(value):
    high = value.astype(BF16)
    low = (value - high.astype(F32)).astype(BF16)
    return high, low


def product(left_tiles, right_tiles):
    left = jnp.concatenate(left_tiles, 1) if len(left_tiles) > 1 else left_tiles[0]
    right = jnp.concatenate(right_tiles, 0) if len(right_tiles) > 1 else right_tiles[0]
    return jnp.dot(left, right, preferred_element_type=F32)


def folded(value):
    rows = value.shape[0] // 2
    return value[:rows] + value[rows:]


def folded_halves(value):
    rows = value.shape[0] // 2
    return jnp.concatenate([folded(value[:rows]), folded(value[rows:])], 0)


class Plane:
    def __init__(self, source, held, send, recv, local, at):
        self.source, self.held, self.send, self.recv, self.local = source, held, send, recv, local
        self.x, self.y, self.c = at
        self.rows = source.shape[0]
        self.half = self.rows // 2
        self.quarter = self.half // 2
        self.started = []

    def device(self, x, y):
        return (wrap(x, 4) * 4 + wrap(y, 4), self.c)

    def targets(self, first):
        x, y = self.x, self.y
        along_x = [self.device(x + 1, y), self.device(x - 1, y)]
        along_y = [self.device(x, y + 1), self.device(x, y - 1)]
        return along_x + along_y if first else along_y + along_x

    def go(self, stage, lane, src, dst, device):
        copy = remote(src, dst, self.send.at[stage, lane], self.recv.at[stage, lane], device)
        copy.start()
        self.started.append(copy)

    def arrive(self, stage, lane, dst):
        remote(dst, dst, self.send.at[stage, lane], self.recv.at[stage, lane], self.device(self.x, self.y + 1)).wait_recv()

    def near(self, lane):
        x, y, held, half, rows = self.x, self.y, self.held, self.half, self.rows
        return [
            held.at[wrap(x - 1, 4), y, 0:half],
            held.at[wrap(x + 1, 4), y, 0:half],
            held.at[x, wrap(y - 1, 4), half:rows],
            held.at[x, wrap(y + 1, 4), half:rows],
        ][lane]

    def open(self):
        self.own = pltpu.make_async_copy(self.source, self.held.at[self.x, self.y], self.local)
        for lane, device in enumerate(self.targets(True)):
            part = slice(0, self.half) if lane < 2 else slice(self.half, self.rows)
            self.go(0, lane, self.source.at[part], self.held.at[self.x, self.y, part], device)
        self.own.start()

    def cross(self):
        x, y, held, half, quarter, rows = self.x, self.y, self.held, self.half, self.quarter, self.rows
        parts = [
            held.at[wrap(x - 1, 4), y, 0:quarter],
            held.at[wrap(x + 1, 4), y, quarter:half],
            held.at[x, wrap(y - 1, 4), half:half + quarter],
            held.at[x, wrap(y + 1, 4), half + quarter:rows],
        ]
        for lane, device in enumerate(self.targets(True)):
            self.arrive(0, lane, self.near(lane))
            self.go(1, lane, parts[lane], parts[lane], device)

    def spread(self):
        x, y, held, half, quarter, rows = self.x, self.y, self.held, self.half, self.quarter, self.rows
        far_x, far_y = wrap(x + 2, 4), wrap(y + 2, 4)
        for lane, part in enumerate([
            held.at[far_x, y, 0:quarter],
            held.at[far_x, y, quarter:half],
            held.at[x, far_y, half:half + quarter],
            held.at[x, far_y, half + quarter:rows],
        ]):
            self.arrive(1, lane, part)
        self.own.wait()
        line_x, line_y = held.at[:, y, 0:half], held.at[x, :, half:rows]
        for lane, device in enumerate(self.targets(False)):
            part = line_x if lane < 2 else line_y
            self.go(2, lane, part, part, device)

    def close(self):
        x, y, held, half, rows = self.x, self.y, self.held, self.half, self.rows
        whole = [
            held.at[:, wrap(y - 1, 4), 0:half],
            held.at[:, wrap(y + 1, 4), 0:half],
            held.at[wrap(x - 1, 4), :, half:rows],
            held.at[wrap(x + 1, 4), :, half:rows],
        ]
        parts = [
            held.at[0:2, wrap(y - 1, 4), 0:half],
            held.at[2:4, wrap(y + 1, 4), 0:half],
            held.at[wrap(x - 1, 4), 0:2, half:rows],
            held.at[wrap(x + 1, 4), 2:4, half:rows],
        ]
        for lane, device in enumerate(self.targets(False)):
            self.arrive(2, lane, whole[lane])
            self.go(3, lane, parts[lane], parts[lane], device)

    def finish(self):
        x, y, held, half, rows = self.x, self.y, self.held, self.half, self.rows
        far_x, far_y = wrap(x + 2, 4), wrap(y + 2, 4)
        for lane, part in enumerate([
            held.at[0:2, far_y, 0:half],
            held.at[2:4, far_y, 0:half],
            held.at[far_x, 0:2, half:rows],
            held.at[far_x, 2:4, half:rows],
        ]):
            self.arrive(3, lane, part)

    def block(self, start, width, tile):
        per_tile = 256 // width
        found = []
        for piece in range(per_tile):
            run = tile * per_tile + piece
            found.append(self.held[run // 4, run % 4, start:start + width])
        return found


class Ring:
    def __init__(self, source, held, send, recv, partner_send, partner_recv, local, at):
        self.source, self.held, self.send, self.recv = source, held, send, recv
        self.partner_send, self.partner_recv, self.local = partner_send, partner_recv, local
        self.r, self.z, self.core = at
        self.started = []

    def slot(self, z, core):
        return self.held.at[wrap(z, 8) * 2 + core, 0:256]

    def device(self, z, core):
        return (self.r, wrap(z, 8) * 2 + core)

    def go(self, step, lane, src, dst):
        shift = 1 if lane == 0 else -1
        copy = remote(src, dst, self.send.at[step, lane], self.recv.at[step, lane], self.device(self.z + shift, self.core))
        copy.start()
        self.started.append(copy)

    def share(self, index, src, dst):
        copy = remote(src, dst, self.partner_send.at[index], self.partner_recv.at[index], self.device(self.z, 1 - self.core))
        copy.start()
        self.started.append(copy)

    def arrive(self, step, lane, dst):
        remote(dst, dst, self.send.at[step, lane], self.recv.at[step, lane], self.device(self.z + 1, self.core)).wait_recv()

    def open(self):
        own = self.slot(self.z, self.core)
        for lane in range(2):
            self.go(0, lane, self.source, own)
        self.share(0, self.source, own)
        self.own = pltpu.make_async_copy(self.source, own, self.local)
        self.own.start()

    def step(self, number):
        for lane in range(2):
            distance = -number if lane == 0 else number
            tile = self.slot(self.z + distance, self.core)
            self.arrive(number - 1, lane, tile)
            if number < 3:
                self.go(number, lane, tile, tile)
            else:
                part = self.held.at[wrap(self.z + distance, 8) * 2 + self.core, 128 * lane:128 * lane + 128]
                self.go(number, lane, part, part)
            self.share(2 * number - 1 + lane, tile, tile)

    def finish(self):
        far = wrap(self.z + 4, 8) * 2 + self.core
        for lane in range(2):
            self.arrive(3, lane, self.held.at[far, 128 * lane:128 * lane + 128])
        tile = self.slot(self.z + 4, self.core)
        self.share(7, tile, tile)
        other = 1 - self.core
        for index, distance in enumerate([0, -1, 1, -2, 2, -3, 3, 4]):
            tile = self.slot(self.z + distance, other)
            remote(tile, tile, self.partner_send.at[index], self.partner_recv.at[index], self.device(self.z, other)).wait_recv()
        self.own.wait()


class Node:
    def __init__(self, held, rows, chips, send, recv, partner_send, partner_recv, at):
        self.held, self.rows, self.chips = held, rows, chips
        self.send, self.recv, self.partner_send, self.partner_recv = send, recv, partner_send, partner_recv
        self.r, self.z, self.core = at
        self.first = self.z - lax.rem(self.z, chips)
        self.place = lax.rem(self.z, chips)
        self.started = []

    def slot(self, place, core):
        return self.held.at[place * 2 + core, self.rows]

    def share(self, index, tile):
        copy = remote(tile, tile, self.partner_send.at[index], self.partner_recv.at[index],
                      (self.r, self.z * 2 + 1 - self.core))
        copy.start()
        self.started.append(copy)

    def open(self):
        tile = self.slot(self.place, self.core)
        for hop in range(1, self.chips):
            target = wrap(self.place + hop, self.chips)
            copy = remote(tile, tile, self.send.at[hop], self.recv.at[hop], (self.r, (self.first + target) * 2 + self.core))
            copy.start()
            self.started.append(copy)
        self.share(0, tile)

    def relay(self):
        for hop in range(1, self.chips):
            tile = self.slot(wrap(self.place - hop, self.chips), self.core)
            remote(tile, tile, self.send.at[hop], self.recv.at[hop], (self.r, self.z * 2 + 1 - self.core)).wait_recv()
            self.share(hop, tile)

    def finish(self):
        other = 1 - self.core
        for hop in range(self.chips):
            tile = self.slot(wrap(self.place - hop, self.chips), other)
            remote(tile, tile, self.partner_send.at[hop], self.partner_recv.at[hop], (self.r, self.z * 2 + other)).wait_recv()


class Chain:
    def __init__(self, held, rows, send, recv, partner_send, partner_recv, at):
        self.held, self.rows = held, rows
        self.send, self.recv, self.partner_send, self.partner_recv = send, recv, partner_send, partner_recv
        self.r, self.z, self.core = at
        self.first = self.z - lax.rem(self.z, 4)
        place = lax.rem(self.z, 4)
        upper, odd = lax.div(place, 2), lax.rem(place, 2)
        self.beside, self.across = place + 1 - 2 * odd, 3 - place
        self.inner = (upper + odd) == 1
        self.order = [place, self.beside, 2 - upper, 3 - 3 * upper]
        self.started, self.started_inner = [], []

    def slot(self, place, core):
        return self.held.at[place * 2 + core, self.rows]

    def copy(self, index, lane, place, target):
        tile = self.slot(place, self.core)
        return remote(tile, tile, self.send.at[index], self.recv.at[lane], (self.r, (self.first + target) * 2 + self.core))

    def share(self, index):
        tile = self.slot(self.order[index], self.core)
        copy = remote(tile, tile, self.partner_send.at[index], self.partner_recv.at[index],
                      (self.r, self.z * 2 + 1 - self.core))
        copy.start()
        self.started.append(copy)

    def inward(self, copy):
        self.started_inner.append(copy)

        @pl.when(self.inner)
        def _():
            copy.start()

    def open(self):
        self.inward(self.copy(1, 1, self.order[0], self.across))
        copy = self.copy(0, 0, self.order[0], self.beside)
        copy.start()
        self.started.append(copy)
        self.share(0)

    def relay(self):
        targets = [self.across, self.beside, self.beside]
        lanes = [2, 1, 2]
        for lane in range(3):
            tile = self.slot(self.order[lane + 1], self.core)
            remote(tile, tile, self.send.at[0], self.recv.at[lane], (self.r, self.z * 2 + 1 - self.core)).wait_recv()
            self.inward(self.copy(2 + lane, lanes[lane], self.order[lane + 1], targets[lane]))
            self.share(lane + 1)

    def finish(self):
        other = 1 - self.core
        for index in range(4):
            tile = self.slot(self.order[index], other)
            remote(tile, tile, self.partner_send.at[index], self.partner_recv.at[index], (self.r, self.z * 2 + other)).wait_recv()

    def drain(self):
        @pl.when(self.inner)
        def _():
            for copy in self.started_inner:
                copy.wait_send()


class Turn:
    def __init__(self, source, place, send, recv, partner_send, partner_recv, local, at):
        self.source, self.place = source, place
        self.send, self.recv, self.partner_send, self.partner_recv, self.local = send, recv, partner_send, partner_recv, local
        self.r, self.c, self.core = at
        self.started = []

    def open(self):
        self.own = pltpu.make_async_copy(self.source.at[self.r], self.place(self.r, self.core), self.local)
        self.own.start()
        for hop in range(1, 16):
            target = wrap(self.r + hop, 16)
            copy = remote(self.source.at[target], self.place(self.r, self.core), self.send.at[hop], self.recv.at[hop], (target, self.c))
            copy.start()
            self.started.append(copy)

    def share(self, hop):
        part = self.place(wrap(self.r - hop, 16), self.core)
        copy = remote(part, part, self.partner_send.at[hop], self.partner_recv.at[hop], (self.r, self.c + 1 - 2 * self.core))
        copy.start()
        self.started.append(copy)

    def relay(self):
        self.own.wait()
        self.share(0)
        for hop in range(1, 16):
            part = self.place(wrap(self.r - hop, 16), self.core)
            remote(part, part, self.send.at[hop], self.recv.at[hop], (wrap(self.r + 1, 16), self.c)).wait_recv()
            self.share(hop)

    def finish(self):
        for hop in range(16):
            part = self.place(wrap(self.r - hop, 16), 1 - self.core)
            remote(part, part, self.partner_send.at[hop], self.partner_recv.at[hop],
                   (self.r, self.c + 1 - 2 * self.core)).wait_recv()


def kernel(root_in, l_one_in, l_two_in, l_three_in, d_one_in, d_two_in, d_three_in, out_one, out_two, out_three,
           root, l_one, l_two, l_three, d_one, d_two, d_three, p_zero, p_one, p_two, p_three, g_one, g_two, g_three, turn_one, turn_two, turn_cross, sums, gained,
           plane_send, plane_recv, ring_send, ring_recv, ring_core_send, ring_core_recv,
           node_send, node_recv, node_core_send, node_core_recv,
           chain_send, chain_recv, chain_core_send, chain_core_recv, swap_send, swap_recv,
           turn_send, turn_recv, turn_core_send, turn_core_recv, last_send, last_recv, local, fetched):
    r, c = lax.axis_index("row"), lax.axis_index("col")
    x, y = lax.div(r, 4), lax.rem(r, 4)
    z, core = lax.div(c, 2), lax.rem(c, 2)
    eighth, quarter = lax.rem(c, 8), lax.rem(c, 4)

    fetches = [
        pltpu.make_async_copy(source, held, fetched.at[index])
        for index, (source, held) in enumerate([
            (l_one_in, l_one), (root_in, root), (l_two_in, l_two), (l_three_in, l_three),
            (d_one_in, d_one), (d_two_in, d_two), (d_three_in, d_three),
        ])
    ]
    for fetch in fetches:
        fetch.start()

    barrier = pltpu.get_barrier_semaphore()
    for hop in range(1, 16):
        pl.semaphore_signal(barrier, inc=1, device_id=(wrap(r + hop, 16), c), device_id_type=MESH)
    for hop in range(1, 8):
        pl.semaphore_signal(barrier, inc=1, device_id=(r, wrap(z + hop, 8) * 2 + core), device_id_type=MESH)
    pl.semaphore_signal(barrier, inc=1, device_id=(r, z * 2 + 1 - core), device_id_type=MESH)
    pl.semaphore_wait(barrier, 23)
    for fetch in fetches:
        fetch.wait()

    planes = [
        Plane(source, held, plane_send.at[level], plane_recv.at[level], local.at[level], (x, y, c))
        for level, (source, held) in enumerate([(l_one, g_one), (l_two, g_two), (l_three, g_three)])
    ]
    one, two, three = planes
    ring = Ring(root, p_zero, ring_send, ring_recv, ring_core_send, ring_core_recv, local.at[3], (r, z, core))

    def node(index, held, rows, chips):
        return Node(held, rows, chips, node_send.at[index], node_recv.at[index], node_core_send.at[index],
                    node_core_recv.at[index], (r, z, core))

    def chain(index, held, rows):
        return Chain(held, rows, chain_send.at[index], chain_recv.at[index], chain_core_send.at[index],
                     chain_core_recv.at[index], (r, z, core))

    s01 = [chain(0, p_one, slice(0, 256)), chain(1, p_one, slice(256, 512))]
    s11 = chain(2, p_one, slice(512, 768))
    s02 = node(0, p_two, slice(0, 512), 2)
    s12 = node(1, p_two, slice(512, 768), 2)
    s22 = node(2, p_two, slice(768, 896), 2)

    def turn(index, source, place):
        return Turn(source, place, turn_send.at[index], turn_recv.at[index], turn_core_send.at[index],
                    turn_core_recv.at[index], local.at[4 + index], (r, c, core))

    def rows_at(start, size, which):
        return pl.ds(pl.multiple_of(start + size * which, size), size)

    def half_turn(half):
        lanes = slice(128 * half, 128 * half + 128)
        return turn(2 + half, turn_one.at[half], lambda run, which: p_zero.at[run, rows_at(256, 128, which), lanes])

    t01 = [half_turn(0), half_turn(1)]
    t02 = turn(0, turn_two, lambda run, which: p_zero.at[run, rows_at(512, 64, which)])
    t12 = turn(1, turn_cross,
               lambda run, which: p_one.at[lax.div(run, 2), rows_at(768, 64, which),
                                           pl.ds(pl.multiple_of(lax.rem(run, 2) * 128, 128), 128)])

    def store(held, index, start, value):
        rows = value.shape[0]
        high, low = halves(value)
        held[index, start:start + rows] = high
        held[index, start + rows:start + 2 * rows] = low

    def zero_part(plane, first, last):
        return product([p_zero[k, first:last] for k in range(16)],
                       [piece for k in range(16) for piece in plane.block(0, 256, k)])

    def one_part(plane, first, last):
        return product([p_one[k, first:last] for k in range(8)],
                       [piece for k in range(8) for piece in plane.block(256, 128, k)])

    def two_part(plane, first, last):
        return product([p_two[k, first:last] for k in range(4)],
                       [piece for k in range(4) for piece in plane.block(384, 64, k)])

    one.open()
    ring.open()
    one.cross()
    ring.step(1)
    one.spread()
    two.open()
    ring.step(2)
    one.close()
    two.cross()
    three.open()
    ring.step(3)
    one.finish()
    two.spread()
    three.cross()
    ring.finish()

    for half in range(2):
        value = -zero_part(one, 128 * half, 128 * half + 128)
        store(p_one, eighth, 256 * half, value)
        s01[half].open()
        out_one[0, 128 * half:128 * half + 128] = value

    two.close()
    three.spread()
    for half in range(2):
        s01[half].relay()
        s01[half].finish()
        for k in range(8):
            tile = p_one[k, rows_at(256 * half, 128, core)]
            turned = tile.T
            turn_one[half, 2 * k] = turned[0:128]
            turn_one[half, 2 * k + 1] = turned[128:256]
        t01[half].open()

    two.finish()
    value = -(zero_part(two, 0, 256) + folded_halves(one_part(two, 0, 512)))
    store(p_two, quarter, 0, value)
    s02.open()
    out_two[0, 0:256] = value

    for half in range(2):
        t01[half].relay()
    for half in range(2):
        t01[half].finish()
    value = d_one[...].astype(F32) - folded(zero_part(one, 256, 512))
    store(p_one, eighth, 512, value)
    s11.open()
    out_one[0, 256:384] = value

    three.close()
    s02.relay()
    s02.finish()
    for k in range(4):
        tile = p_two[k, rows_at(0, 256, core)]
        turned = tile.T
        for piece in range(4):
            turn_two[4 * k + piece] = turned[64 * piece:64 * piece + 64]
    t02.open()

    s11.relay()
    s11.finish()
    value = -folded(zero_part(two, 256, 512) + one_part(two, 512, 768))
    store(p_two, quarter, 512, value)
    s12.open()
    out_two[0, 256:384] = value

    s12.relay()
    s12.finish()
    for k in range(4):
        tile = p_two[k, rows_at(512, 128, core)]
        turned = tile.T
        for piece in range(4):
            turn_cross[4 * k + piece] = turned[64 * piece:64 * piece + 64]
    t12.open()

    three.finish()
    upper = -(zero_part(three, 0, 256) + folded_halves(one_part(three, 0, 512)) + folded(two_part(three, 0, 512)))
    out_three[0, 0:256] = upper
    high, low = halves(upper)
    p_three[core, 0:256] = high
    p_three[core, 384:640] = low
    middle = -folded(zero_part(three, 256, 512) + one_part(three, 512, 768) + two_part(three, 512, 768))
    out_three[0, 256:384] = middle
    high, low = halves(middle)
    p_three[core, 256:384] = high
    p_three[core, 640:768] = low

    def swapped(index, rows):
        mine, theirs = p_three.at[core, rows], p_three.at[1 - core, rows]
        device = (r, z * 2 + 1 - core)
        return (remote(mine, mine, swap_send.at[index], swap_recv.at[index], device),
                remote(theirs, theirs, swap_send.at[index], swap_recv.at[index], device))

    def inner_terms(which, start, size, factor):
        turned = jnp.concatenate([p_three[which, start:start + size].T, p_three[which, start + size:start + 2 * size].T], 0)
        return folded(jnp.dot(turned, factor, preferred_element_type=F32))

    first_swap, first_gain = swapped(0, slice(0, 768))
    first_swap.start()

    t02.relay()
    t12.relay()
    t02.finish()
    t12.finish()
    value = d_two[...].astype(F32) - folded(zero_part(two, 512, 640) + one_part(two, 768, 896))
    store(p_two, quarter, 768, value)
    s22.open()
    out_two[0, 384:448] = value
    first_gain.wait_recv()
    for which in range(2):
        partial = inner_terms(which, 0, 384, l_three[0:384])
        for piece in range(8):
            sums[8 * which + piece] = partial[32 * piece:32 * piece + 32]
    s22.relay()
    s22.finish()

    lower = -folded(zero_part(three, 512, 640) + one_part(three, 768, 896) + two_part(three, 768, 896))
    high, low = halves(lower)
    p_three[core, 768:832] = high
    p_three[core, 832:896] = low
    last_swap, last_gain = swapped(1, slice(768, 896))
    last_swap.start()
    out_three[0, 384:448] = lower
    last_gain.wait_recv()
    for which in range(2):
        partial = inner_terms(which, 768, 64, l_three[384:448])
        for piece in range(8):
            sums[8 * which + piece] = sums[8 * which + piece] + partial[32 * piece:32 * piece + 32]
    final = []
    for hop in range(1, 16):
        target = wrap(r + hop, 16)
        copy = remote(sums.at[target], gained.at[r], last_send.at[hop], last_recv.at[hop], (target, c))
        copy.start()
        final.append(copy)
    total = sums[r]
    for hop in range(1, 16):
        source = wrap(r - hop, 16)
        part = gained.at[source]
        remote(part, part, last_send.at[hop], last_recv.at[hop], (wrap(r + 1, 16), c)).wait_recv()
        total = total + gained[source]
    out_three[0, 448:480] = d_three[...].astype(F32) - total

    first_swap.wait_send()
    last_swap.wait_send()
    for group in [one, two, three, ring, *s01, s11, s02, s12, s22, *t01, t02, t12]:
        for copy in group.started:
            copy.wait_send()
    for group in [*s01, s11]:
        group.drain()
    for copy in final:
        copy.wait_send()


def per_device(root_block, l_one, dinv_one, l_two, dinv_two, l_three, dinv_three):
    vmem = pl.BlockSpec(memory_space=pltpu.VMEM)
    dma = pltpu.SemaphoreType.DMA
    return pl.pallas_call(
        kernel,
        out_shape=(
            pltpu.VMEM((1, 384, 256), F32),
            pltpu.VMEM((1, 448, 256), F32),
            pltpu.VMEM((1, 480, 256), F32),
        ),
        in_specs=[pl.BlockSpec(memory_space=pl.ANY)] * 7,
        out_specs=(vmem, vmem, vmem),
        scratch_shapes=[
            pltpu.VMEM((256, 256), BF16),
            pltpu.VMEM((256, 256), BF16),
            pltpu.VMEM((384, 256), BF16),
            pltpu.VMEM((448, 256), BF16),
            pltpu.VMEM((128, 256), BF16),
            pltpu.VMEM((64, 256), BF16),
            pltpu.VMEM((32, 256), BF16),
            pltpu.VMEM((16, 640, 256), BF16),
            pltpu.VMEM((8, 896, 256), BF16),
            pltpu.VMEM((4, 896, 256), BF16),
            pltpu.VMEM((2, 896, 256), BF16),
            pltpu.VMEM((4, 4, 256, 256), BF16),
            pltpu.VMEM((4, 4, 384, 256), BF16),
            pltpu.VMEM((4, 4, 448, 256), BF16),
            pltpu.VMEM((2, 16, 128, 128), BF16),
            pltpu.VMEM((16, 64, 256), BF16),
            pltpu.VMEM((16, 64, 128), BF16),
            pltpu.VMEM((16, 32, 256), F32),
            pltpu.VMEM((16, 32, 256), F32),
            dma((3, 4, 4)), dma((3, 4, 4)),
            dma((4, 2)), dma((4, 2)), dma((8,)), dma((8,)),
            dma((3, 2)), dma((3, 2)), dma((3, 2)), dma((3, 2)),
            dma((3, 5)), dma((3, 3)), dma((3, 4)), dma((3, 4)), dma((2,)), dma((2,)),
            dma((4, 16)), dma((4, 16)), dma((4, 16)), dma((4, 16)),
            dma((16,)), dma((16,)),
            dma((8,)), dma((7,)),
        ],
        compiler_params=pltpu.CompilerParams(
            collective_id=0, has_side_effects=True, vmem_limit_bytes=60 * 1024 * 1024
        ),
    )(root_block[0], l_one[0], l_two[0], l_three[0], dinv_one[0], dinv_two[0], dinv_three[0])


def solution(mesh):
    placed = (P("row", None, "col"),) * 7
    return jax.shard_map(
        per_device,
        mesh=mesh,
        in_specs=placed,
        out_specs=(P("row", None, "col"), P("row", None, "col"), P("row", None, "col")),
        check_vma=False,
    )
```

```python
import jax
import jax.numpy as jnp
from jax import lax
from jax.experimental import pallas as pl
from jax.experimental.pallas import tpu as pltpu
from jax.sharding import PartitionSpec as P

MESH = pl.DeviceIdType.MESH
F32 = jnp.float32
BF16 = jnp.bfloat16


def wrap(value, extent):
    return lax.rem(value + extent, extent)


def remote(src, dst, send_sem, recv_sem, device):
    return pltpu.make_async_remote_copy(
        src_ref=src, dst_ref=dst, send_sem=send_sem, recv_sem=recv_sem,
        device_id=device, device_id_type=MESH,
    )


def halves(value):
    high = value.astype(BF16)
    low = (value - high.astype(F32)).astype(BF16)
    return high, low


def product(left_tiles, right_tiles):
    left = jnp.concatenate(left_tiles, 1) if len(left_tiles) > 1 else left_tiles[0]
    right = jnp.concatenate(right_tiles, 0) if len(right_tiles) > 1 else right_tiles[0]
    return jnp.dot(left, right, preferred_element_type=F32)


def folded(value):
    rows = value.shape[0] // 2
    return value[:rows] + value[rows:]


def folded_halves(value):
    rows = value.shape[0] // 2
    return jnp.concatenate([folded(value[:rows]), folded(value[rows:])], 0)


class Plane:
    def __init__(self, source, held, send, recv, local, at):
        self.source, self.held, self.send, self.recv, self.local = source, held, send, recv, local
        self.x, self.y, self.c = at
        self.rows = source.shape[0]
        self.half = self.rows // 2
        self.quarter = self.half // 2
        self.started = []

    def device(self, x, y):
        return (wrap(x, 4) * 4 + wrap(y, 4), self.c)

    def targets(self, first):
        x, y = self.x, self.y
        along_x = [self.device(x + 1, y), self.device(x - 1, y)]
        along_y = [self.device(x, y + 1), self.device(x, y - 1)]
        return along_x + along_y if first else along_y + along_x

    def go(self, stage, lane, src, dst, device):
        copy = remote(src, dst, self.send.at[stage, lane], self.recv.at[stage, lane], device)
        copy.start()
        self.started.append(copy)

    def arrive(self, stage, lane, dst):
        remote(dst, dst, self.send.at[stage, lane], self.recv.at[stage, lane], self.device(self.x, self.y + 1)).wait_recv()

    def near(self, lane):
        x, y, held, half, rows = self.x, self.y, self.held, self.half, self.rows
        return [
            held.at[wrap(x - 1, 4), y, 0:half],
            held.at[wrap(x + 1, 4), y, 0:half],
            held.at[x, wrap(y - 1, 4), half:rows],
            held.at[x, wrap(y + 1, 4), half:rows],
        ][lane]

    def open(self):
        self.own = pltpu.make_async_copy(self.source, self.held.at[self.x, self.y], self.local)
        for lane, device in enumerate(self.targets(True)):
            part = slice(0, self.half) if lane < 2 else slice(self.half, self.rows)
            self.go(0, lane, self.source.at[part], self.held.at[self.x, self.y, part], device)
        self.own.start()

    def cross(self):
        x, y, held, half, quarter, rows = self.x, self.y, self.held, self.half, self.quarter, self.rows
        parts = [
            held.at[wrap(x - 1, 4), y, 0:quarter],
            held.at[wrap(x + 1, 4), y, quarter:half],
            held.at[x, wrap(y - 1, 4), half:half + quarter],
            held.at[x, wrap(y + 1, 4), half + quarter:rows],
        ]
        for lane, device in enumerate(self.targets(True)):
            self.arrive(0, lane, self.near(lane))
            self.go(1, lane, parts[lane], parts[lane], device)

    def spread(self):
        x, y, held, half, quarter, rows = self.x, self.y, self.held, self.half, self.quarter, self.rows
        far_x, far_y = wrap(x + 2, 4), wrap(y + 2, 4)
        for lane, part in enumerate([
            held.at[far_x, y, 0:quarter],
            held.at[far_x, y, quarter:half],
            held.at[x, far_y, half:half + quarter],
            held.at[x, far_y, half + quarter:rows],
        ]):
            self.arrive(1, lane, part)
        self.own.wait()
        line_x, line_y = held.at[:, y, 0:half], held.at[x, :, half:rows]
        for lane, device in enumerate(self.targets(False)):
            part = line_x if lane < 2 else line_y
            self.go(2, lane, part, part, device)

    def close(self):
        x, y, held, half, rows = self.x, self.y, self.held, self.half, self.rows
        whole = [
            held.at[:, wrap(y - 1, 4), 0:half],
            held.at[:, wrap(y + 1, 4), 0:half],
            held.at[wrap(x - 1, 4), :, half:rows],
            held.at[wrap(x + 1, 4), :, half:rows],
        ]
        parts = [
            held.at[0:2, wrap(y - 1, 4), 0:half],
            held.at[2:4, wrap(y + 1, 4), 0:half],
            held.at[wrap(x - 1, 4), 0:2, half:rows],
            held.at[wrap(x + 1, 4), 2:4, half:rows],
        ]
        for lane, device in enumerate(self.targets(False)):
            self.arrive(2, lane, whole[lane])
            self.go(3, lane, parts[lane], parts[lane], device)

    def finish(self):
        x, y, held, half, rows = self.x, self.y, self.held, self.half, self.rows
        far_x, far_y = wrap(x + 2, 4), wrap(y + 2, 4)
        for lane, part in enumerate([
            held.at[0:2, far_y, 0:half],
            held.at[2:4, far_y, 0:half],
            held.at[far_x, 0:2, half:rows],
            held.at[far_x, 2:4, half:rows],
        ]):
            self.arrive(3, lane, part)

    def block(self, start, width, tile):
        per_tile = 256 // width
        found = []
        for piece in range(per_tile):
            run = tile * per_tile + piece
            found.append(self.held[run // 4, run % 4, start:start + width])
        return found


class Ring:
    def __init__(self, source, held, send, recv, partner_send, partner_recv, local, at):
        self.source, self.held, self.send, self.recv = source, held, send, recv
        self.partner_send, self.partner_recv, self.local = partner_send, partner_recv, local
        self.r, self.z, self.core = at
        self.started = []

    def slot(self, z, core):
        return self.held.at[wrap(z, 8) * 2 + core, 0:256]

    def device(self, z, core):
        return (self.r, wrap(z, 8) * 2 + core)

    def go(self, step, lane, src, dst):
        shift = 1 if lane == 0 else -1
        copy = remote(src, dst, self.send.at[step, lane], self.recv.at[step, lane], self.device(self.z + shift, self.core))
        copy.start()
        self.started.append(copy)

    def share(self, index, src, dst):
        copy = remote(src, dst, self.partner_send.at[index], self.partner_recv.at[index], self.device(self.z, 1 - self.core))
        copy.start()
        self.started.append(copy)

    def arrive(self, step, lane, dst):
        remote(dst, dst, self.send.at[step, lane], self.recv.at[step, lane], self.device(self.z + 1, self.core)).wait_recv()

    def open(self):
        own = self.slot(self.z, self.core)
        for lane in range(2):
            self.go(0, lane, self.source, own)
        self.share(0, self.source, own)
        self.own = pltpu.make_async_copy(self.source, own, self.local)
        self.own.start()

    def step(self, number):
        for lane in range(2):
            distance = -number if lane == 0 else number
            tile = self.slot(self.z + distance, self.core)
            self.arrive(number - 1, lane, tile)
            if number < 3:
                self.go(number, lane, tile, tile)
            else:
                part = self.held.at[wrap(self.z + distance, 8) * 2 + self.core, 128 * lane:128 * lane + 128]
                self.go(number, lane, part, part)
            self.share(2 * number - 1 + lane, tile, tile)

    def finish(self):
        far = wrap(self.z + 4, 8) * 2 + self.core
        for lane in range(2):
            self.arrive(3, lane, self.held.at[far, 128 * lane:128 * lane + 128])
        tile = self.slot(self.z + 4, self.core)
        self.share(7, tile, tile)
        other = 1 - self.core
        for index, distance in enumerate([0, -1, 1, -2, 2, -3, 3, 4]):
            tile = self.slot(self.z + distance, other)
            remote(tile, tile, self.partner_send.at[index], self.partner_recv.at[index], self.device(self.z, other)).wait_recv()
        self.own.wait()


class Node:
    def __init__(self, held, rows, chips, send, recv, partner_send, partner_recv, at):
        self.held, self.rows, self.chips = held, rows, chips
        self.send, self.recv, self.partner_send, self.partner_recv = send, recv, partner_send, partner_recv
        self.r, self.z, self.core = at
        self.first = self.z - lax.rem(self.z, chips)
        self.place = lax.rem(self.z, chips)
        self.started = []

    def slot(self, place, core):
        return self.held.at[place * 2 + core, self.rows]

    def share(self, index, tile):
        copy = remote(tile, tile, self.partner_send.at[index], self.partner_recv.at[index],
                      (self.r, self.z * 2 + 1 - self.core))
        copy.start()
        self.started.append(copy)

    def open(self):
        tile = self.slot(self.place, self.core)
        for hop in range(1, self.chips):
            target = wrap(self.place + hop, self.chips)
            copy = remote(tile, tile, self.send.at[hop], self.recv.at[hop], (self.r, (self.first + target) * 2 + self.core))
            copy.start()
            self.started.append(copy)
        self.share(0, tile)

    def relay(self):
        for hop in range(1, self.chips):
            tile = self.slot(wrap(self.place - hop, self.chips), self.core)
            remote(tile, tile, self.send.at[hop], self.recv.at[hop], (self.r, self.z * 2 + 1 - self.core)).wait_recv()
            self.share(hop, tile)

    def finish(self):
        other = 1 - self.core
        for hop in range(self.chips):
            tile = self.slot(wrap(self.place - hop, self.chips), other)
            remote(tile, tile, self.partner_send.at[hop], self.partner_recv.at[hop], (self.r, self.z * 2 + other)).wait_recv()


class Chain:
    def __init__(self, held, rows, send, recv, partner_send, partner_recv, at):
        self.held, self.rows = held, rows
        self.send, self.recv, self.partner_send, self.partner_recv = send, recv, partner_send, partner_recv
        self.r, self.z, self.core = at
        self.first = self.z - lax.rem(self.z, 4)
        place = lax.rem(self.z, 4)
        upper, odd = lax.div(place, 2), lax.rem(place, 2)
        self.beside, self.across = place + 1 - 2 * odd, 3 - place
        self.inner = (upper + odd) == 1
        self.order = [place, self.beside, 2 - upper, 3 - 3 * upper]
        self.started, self.started_inner = [], []

    def slot(self, place, core):
        return self.held.at[place * 2 + core, self.rows]

    def copy(self, index, lane, place, target):
        tile = self.slot(place, self.core)
        return remote(tile, tile, self.send.at[index], self.recv.at[lane], (self.r, (self.first + target) * 2 + self.core))

    def share(self, index):
        tile = self.slot(self.order[index], self.core)
        copy = remote(tile, tile, self.partner_send.at[index], self.partner_recv.at[index],
                      (self.r, self.z * 2 + 1 - self.core))
        copy.start()
        self.started.append(copy)

    def inward(self, copy):
        self.started_inner.append(copy)

        @pl.when(self.inner)
        def _():
            copy.start()

    def open(self):
        self.inward(self.copy(1, 1, self.order[0], self.across))
        copy = self.copy(0, 0, self.order[0], self.beside)
        copy.start()
        self.started.append(copy)
        self.share(0)

    def relay(self):
        targets = [self.across, self.beside, self.beside]
        lanes = [2, 1, 2]
        for lane in range(3):
            tile = self.slot(self.order[lane + 1], self.core)
            remote(tile, tile, self.send.at[0], self.recv.at[lane], (self.r, self.z * 2 + 1 - self.core)).wait_recv()
            self.inward(self.copy(2 + lane, lanes[lane], self.order[lane + 1], targets[lane]))
            self.share(lane + 1)

    def finish(self):
        other = 1 - self.core
        for index in range(4):
            tile = self.slot(self.order[index], other)
            remote(tile, tile, self.partner_send.at[index], self.partner_recv.at[index], (self.r, self.z * 2 + other)).wait_recv()

    def drain(self):
        @pl.when(self.inner)
        def _():
            for copy in self.started_inner:
                copy.wait_send()


class Turn:
    def __init__(self, source, place, send, recv, partner_send, partner_recv, local, at):
        self.source, self.place = source, place
        self.send, self.recv, self.partner_send, self.partner_recv, self.local = send, recv, partner_send, partner_recv, local
        self.r, self.c, self.core = at
        self.started = []

    def open(self):
        self.own = pltpu.make_async_copy(self.source.at[self.r], self.place(self.r, self.core), self.local)
        self.own.start()
        for hop in range(1, 16):
            target = wrap(self.r + hop, 16)
            copy = remote(self.source.at[target], self.place(self.r, self.core), self.send.at[hop], self.recv.at[hop], (target, self.c))
            copy.start()
            self.started.append(copy)

    def share(self, hop):
        part = self.place(wrap(self.r - hop, 16), self.core)
        copy = remote(part, part, self.partner_send.at[hop], self.partner_recv.at[hop], (self.r, self.c + 1 - 2 * self.core))
        copy.start()
        self.started.append(copy)

    def relay(self):
        self.own.wait()
        self.share(0)
        for hop in range(1, 16):
            part = self.place(wrap(self.r - hop, 16), self.core)
            remote(part, part, self.send.at[hop], self.recv.at[hop], (wrap(self.r + 1, 16), self.c)).wait_recv()
            self.share(hop)

    def finish(self):
        for hop in range(16):
            part = self.place(wrap(self.r - hop, 16), 1 - self.core)
            remote(part, part, self.partner_send.at[hop], self.partner_recv.at[hop],
                   (self.r, self.c + 1 - 2 * self.core)).wait_recv()


def kernel(root_in, l_one_in, l_two_in, l_three_in, d_one_in, d_two_in, d_three_in, out_one, out_two, out_three,
           root, l_one, l_two, l_three, d_one, d_two, d_three, p_zero, p_one, p_two, p_three, g_one, g_two, g_three, turn_one, turn_two, turn_cross, sums, gained,
           plane_send, plane_recv, ring_send, ring_recv, ring_core_send, ring_core_recv,
           node_send, node_recv, node_core_send, node_core_recv,
           chain_send, chain_recv, chain_core_send, chain_core_recv, swap_send, swap_recv,
           turn_send, turn_recv, turn_core_send, turn_core_recv, last_send, last_recv, local, fetched):
    r, c = lax.axis_index("row"), lax.axis_index("col")
    x, y = lax.div(r, 4), lax.rem(r, 4)
    z, core = lax.div(c, 2), lax.rem(c, 2)
    eighth, quarter = lax.rem(c, 8), lax.rem(c, 4)

    fetches = [
        pltpu.make_async_copy(source, held, fetched.at[index])
        for index, (source, held) in enumerate([
            (l_one_in, l_one), (root_in, root), (l_two_in, l_two), (l_three_in, l_three),
            (d_one_in, d_one), (d_two_in, d_two), (d_three_in, d_three),
        ])
    ]
    for fetch in fetches:
        fetch.start()

    barrier = pltpu.get_barrier_semaphore()
    for hop in range(1, 16):
        pl.semaphore_signal(barrier, inc=1, device_id=(wrap(r + hop, 16), c), device_id_type=MESH)
    for hop in range(1, 8):
        pl.semaphore_signal(barrier, inc=1, device_id=(r, wrap(z + hop, 8) * 2 + core), device_id_type=MESH)
    pl.semaphore_signal(barrier, inc=1, device_id=(r, z * 2 + 1 - core), device_id_type=MESH)
    pl.semaphore_wait(barrier, 23)
    for fetch in fetches:
        fetch.wait()

    planes = [
        Plane(source, held, plane_send.at[level], plane_recv.at[level], local.at[level], (x, y, c))
        for level, (source, held) in enumerate([(l_one, g_one), (l_two, g_two), (l_three, g_three)])
    ]
    one, two, three = planes
    ring = Ring(root, p_zero, ring_send, ring_recv, ring_core_send, ring_core_recv, local.at[3], (r, z, core))

    def node(index, held, rows, chips):
        return Node(held, rows, chips, node_send.at[index], node_recv.at[index], node_core_send.at[index],
                    node_core_recv.at[index], (r, z, core))

    def chain(index, held, rows):
        return Chain(held, rows, chain_send.at[index], chain_recv.at[index], chain_core_send.at[index],
                     chain_core_recv.at[index], (r, z, core))

    s01 = [chain(0, p_one, slice(0, 256)), chain(1, p_one, slice(256, 512))]
    s11 = chain(2, p_one, slice(512, 768))
    s02 = node(0, p_two, slice(0, 512), 2)
    s12 = node(1, p_two, slice(512, 768), 2)
    s22 = node(2, p_two, slice(768, 896), 2)

    def turn(index, source, place):
        return Turn(source, place, turn_send.at[index], turn_recv.at[index], turn_core_send.at[index],
                    turn_core_recv.at[index], local.at[4 + index], (r, c, core))

    def rows_at(start, size, which):
        return pl.ds(pl.multiple_of(start + size * which, size), size)

    def half_turn(half):
        lanes = slice(128 * half, 128 * half + 128)
        return turn(2 + half, turn_one.at[half], lambda run, which: p_zero.at[run, rows_at(256, 128, which), lanes])

    t01 = [half_turn(0), half_turn(1)]
    t02 = turn(0, turn_two, lambda run, which: p_zero.at[run, rows_at(512, 64, which)])
    t12 = turn(1, turn_cross,
               lambda run, which: p_one.at[lax.div(run, 2), rows_at(768, 64, which),
                                           pl.ds(pl.multiple_of(lax.rem(run, 2) * 128, 128), 128)])

    def store(held, index, start, value):
        rows = value.shape[0]
        high, low = halves(value)
        held[index, start:start + rows] = high
        held[index, start + rows:start + 2 * rows] = low

    def zero_part(plane, first, last):
        return product([p_zero[k, first:last] for k in range(16)],
                       [piece for k in range(16) for piece in plane.block(0, 256, k)])

    def one_part(plane, first, last):
        return product([p_one[k, first:last] for k in range(8)],
                       [piece for k in range(8) for piece in plane.block(256, 128, k)])

    def two_part(plane, first, last):
        return product([p_two[k, first:last] for k in range(4)],
                       [piece for k in range(4) for piece in plane.block(384, 64, k)])

    one.open()
    ring.open()
    one.cross()
    ring.step(1)
    one.spread()
    two.open()
    ring.step(2)
    one.close()
    two.cross()
    three.open()
    ring.step(3)
    one.finish()
    two.spread()
    three.cross()
    ring.finish()

    for half in range(2):
        value = -zero_part(one, 128 * half, 128 * half + 128)
        store(p_one, eighth, 256 * half, value)
        s01[half].open()
        out_one[0, 128 * half:128 * half + 128] = value

    two.close()
    three.spread()
    for half in range(2):
        s01[half].relay()
        s01[half].finish()
        for k in range(8):
            tile = p_one[k, rows_at(256 * half, 128, core)]
            turned = tile.T
            turn_one[half, 2 * k] = turned[0:128]
            turn_one[half, 2 * k + 1] = turned[128:256]
        t01[half].open()

    two.finish()
    value = -(zero_part(two, 0, 256) + folded_halves(one_part(two, 0, 512)))
    store(p_two, quarter, 0, value)
    s02.open()
    out_two[0, 0:256] = value

    for half in range(2):
        t01[half].relay()
    for half in range(2):
        t01[half].finish()
    value = d_one[...].astype(F32) - folded(zero_part(one, 256, 512))
    store(p_one, eighth, 512, value)
    s11.open()
    out_one[0, 256:384] = value

    three.close()
    s02.relay()
    s02.finish()
    for k in range(4):
        tile = p_two[k, rows_at(0, 256, core)]
        turned = tile.T
        for piece in range(4):
            turn_two[4 * k + piece] = turned[64 * piece:64 * piece + 64]
    t02.open()

    early = zero_part(two, 256, 512)
    s11.relay()
    s11.finish()
    value = -folded(early + one_part(two, 512, 768))
    store(p_two, quarter, 512, value)
    s12.open()
    out_two[0, 256:384] = value

    three.finish()
    upper = -(zero_part(three, 0, 256) + folded_halves(one_part(three, 0, 512)) + folded(two_part(three, 0, 512)))
    out_three[0, 0:256] = upper
    high, low = halves(upper)
    p_three[core, 0:256] = high
    p_three[core, 384:640] = low
    early = zero_part(three, 256, 512) + one_part(three, 512, 768)
    s12.relay()
    s12.finish()
    for k in range(4):
        tile = p_two[k, rows_at(512, 128, core)]
        turned = tile.T
        for piece in range(4):
            turn_cross[4 * k + piece] = turned[64 * piece:64 * piece + 64]
    t12.open()

    middle = -folded(early + two_part(three, 512, 768))
    out_three[0, 256:384] = middle
    high, low = halves(middle)
    p_three[core, 256:384] = high
    p_three[core, 640:768] = low

    def swapped(index, rows):
        mine, theirs = p_three.at[core, rows], p_three.at[1 - core, rows]
        device = (r, z * 2 + 1 - core)
        return (remote(mine, mine, swap_send.at[index], swap_recv.at[index], device),
                remote(theirs, theirs, swap_send.at[index], swap_recv.at[index], device))

    def inner_terms(which, start, size, factor):
        turned = jnp.concatenate([p_three[which, start:start + size].T, p_three[which, start + size:start + 2 * size].T], 0)
        return folded(jnp.dot(turned, factor, preferred_element_type=F32))

    first_swap, first_gain = swapped(0, slice(0, 768))
    first_swap.start()

    t02.relay()
    t12.relay()
    t02.finish()
    early = zero_part(two, 512, 640)
    t12.finish()
    value = d_two[...].astype(F32) - folded(early + one_part(two, 768, 896))
    store(p_two, quarter, 768, value)
    s22.open()
    out_two[0, 384:448] = value
    first_gain.wait_recv()
    for which in range(2):
        partial = inner_terms(which, 0, 384, l_three[0:384])
        for piece in range(8):
            sums[8 * which + piece] = partial[32 * piece:32 * piece + 32]
    early = zero_part(three, 512, 640) + one_part(three, 768, 896)
    s22.relay()
    s22.finish()

    lower = -folded(early + two_part(three, 768, 896))
    high, low = halves(lower)
    p_three[core, 768:832] = high
    p_three[core, 832:896] = low
    last_swap, last_gain = swapped(1, slice(768, 896))
    last_swap.start()
    out_three[0, 384:448] = lower
    last_gain.wait_recv()
    for which in range(2):
        partial = inner_terms(which, 768, 64, l_three[384:448])
        for piece in range(8):
            sums[8 * which + piece] = sums[8 * which + piece] + partial[32 * piece:32 * piece + 32]
    final = []
    for hop in range(1, 16):
        target = wrap(r + hop, 16)
        copy = remote(sums.at[target], gained.at[r], last_send.at[hop], last_recv.at[hop], (target, c))
        copy.start()
        final.append(copy)
    total = sums[r]
    for hop in range(1, 16):
        source = wrap(r - hop, 16)
        part = gained.at[source]
        remote(part, part, last_send.at[hop], last_recv.at[hop], (wrap(r + 1, 16), c)).wait_recv()
        total = total + gained[source]
    out_three[0, 448:480] = d_three[...].astype(F32) - total

    first_swap.wait_send()
    last_swap.wait_send()
    for group in [one, two, three, ring, *s01, s11, s02, s12, s22, *t01, t02, t12]:
        for copy in group.started:
            copy.wait_send()
    for group in [*s01, s11]:
        group.drain()
    for copy in final:
        copy.wait_send()


def per_device(root_block, l_one, dinv_one, l_two, dinv_two, l_three, dinv_three):
    vmem = pl.BlockSpec(memory_space=pltpu.VMEM)
    dma = pltpu.SemaphoreType.DMA
    return pl.pallas_call(
        kernel,
        out_shape=(
            pltpu.VMEM((1, 384, 256), F32),
            pltpu.VMEM((1, 448, 256), F32),
            pltpu.VMEM((1, 480, 256), F32),
        ),
        in_specs=[pl.BlockSpec(memory_space=pl.ANY)] * 7,
        out_specs=(vmem, vmem, vmem),
        scratch_shapes=[
            pltpu.VMEM((256, 256), BF16),
            pltpu.VMEM((256, 256), BF16),
            pltpu.VMEM((384, 256), BF16),
            pltpu.VMEM((448, 256), BF16),
            pltpu.VMEM((128, 256), BF16),
            pltpu.VMEM((64, 256), BF16),
            pltpu.VMEM((32, 256), BF16),
            pltpu.VMEM((16, 640, 256), BF16),
            pltpu.VMEM((8, 896, 256), BF16),
            pltpu.VMEM((4, 896, 256), BF16),
            pltpu.VMEM((2, 896, 256), BF16),
            pltpu.VMEM((4, 4, 256, 256), BF16),
            pltpu.VMEM((4, 4, 384, 256), BF16),
            pltpu.VMEM((4, 4, 448, 256), BF16),
            pltpu.VMEM((2, 16, 128, 128), BF16),
            pltpu.VMEM((16, 64, 256), BF16),
            pltpu.VMEM((16, 64, 128), BF16),
            pltpu.VMEM((16, 32, 256), F32),
            pltpu.VMEM((16, 32, 256), F32),
            dma((3, 4, 4)), dma((3, 4, 4)),
            dma((4, 2)), dma((4, 2)), dma((8,)), dma((8,)),
            dma((3, 2)), dma((3, 2)), dma((3, 2)), dma((3, 2)),
            dma((3, 5)), dma((3, 3)), dma((3, 4)), dma((3, 4)), dma((2,)), dma((2,)),
            dma((4, 16)), dma((4, 16)), dma((4, 16)), dma((4, 16)),
            dma((16,)), dma((16,)),
            dma((8,)), dma((7,)),
        ],
        compiler_params=pltpu.CompilerParams(
            collective_id=0, has_side_effects=True, vmem_limit_bytes=60 * 1024 * 1024
        ),
    )(root_block[0], l_one[0], l_two[0], l_three[0], dinv_one[0], dinv_two[0], dinv_three[0])


def solution(mesh):
    placed = (P("row", None, "col"),) * 7
    return jax.shard_map(
        per_device,
        mesh=mesh,
        in_specs=placed,
        out_specs=(P("row", None, "col"), P("row", None, "col"), P("row", None, "col")),
        check_vma=False,
    )
```

```python
import jax
import jax.numpy as jnp
from jax import lax
from jax.experimental import pallas as pl
from jax.experimental.pallas import tpu as pltpu
from jax.sharding import PartitionSpec as P

MESH = pl.DeviceIdType.MESH
F32 = jnp.float32
BF16 = jnp.bfloat16


def wrap(value, extent):
    return lax.rem(value + extent, extent)


def remote(src, dst, send_sem, recv_sem, device):
    return pltpu.make_async_remote_copy(
        src_ref=src, dst_ref=dst, send_sem=send_sem, recv_sem=recv_sem,
        device_id=device, device_id_type=MESH,
    )


def halves(value):
    high = value.astype(BF16)
    low = (value - high.astype(F32)).astype(BF16)
    return high, low


def product(left_tiles, right_tiles):
    left = jnp.concatenate(left_tiles, 1) if len(left_tiles) > 1 else left_tiles[0]
    right = jnp.concatenate(right_tiles, 0) if len(right_tiles) > 1 else right_tiles[0]
    return jnp.dot(left, right, preferred_element_type=F32)


def folded(value):
    rows = value.shape[0] // 2
    return value[:rows] + value[rows:]


def folded_halves(value):
    rows = value.shape[0] // 2
    return jnp.concatenate([folded(value[:rows]), folded(value[rows:])], 0)


class Plane:
    def __init__(self, source, held, send, recv, local, at):
        self.source, self.held, self.send, self.recv, self.local = source, held, send, recv, local
        self.x, self.y, self.c = at
        self.rows = source.shape[0]
        self.half = self.rows // 2
        self.quarter = self.half // 2
        self.started = []

    def device(self, x, y):
        return (wrap(x, 4) * 4 + wrap(y, 4), self.c)

    def targets(self, first):
        x, y = self.x, self.y
        along_x = [self.device(x + 1, y), self.device(x - 1, y)]
        along_y = [self.device(x, y + 1), self.device(x, y - 1)]
        return along_x + along_y if first else along_y + along_x

    def go(self, stage, lane, src, dst, device):
        copy = remote(src, dst, self.send.at[stage, lane], self.recv.at[stage, lane], device)
        copy.start()
        self.started.append(copy)

    def arrive(self, stage, lane, dst):
        remote(dst, dst, self.send.at[stage, lane], self.recv.at[stage, lane], self.device(self.x, self.y + 1)).wait_recv()

    def near(self, lane):
        x, y, held, half, rows = self.x, self.y, self.held, self.half, self.rows
        return [
            held.at[wrap(x - 1, 4), y, 0:half],
            held.at[wrap(x + 1, 4), y, 0:half],
            held.at[x, wrap(y - 1, 4), half:rows],
            held.at[x, wrap(y + 1, 4), half:rows],
        ][lane]

    def open(self):
        self.own = pltpu.make_async_copy(self.source, self.held.at[self.x, self.y], self.local)
        for lane, device in enumerate(self.targets(True)):
            part = slice(0, self.half) if lane < 2 else slice(self.half, self.rows)
            self.go(0, lane, self.source.at[part], self.held.at[self.x, self.y, part], device)
        self.own.start()

    def cross(self):
        x, y, held, half, quarter, rows = self.x, self.y, self.held, self.half, self.quarter, self.rows
        parts = [
            held.at[wrap(x - 1, 4), y, 0:quarter],
            held.at[wrap(x + 1, 4), y, quarter:half],
            held.at[x, wrap(y - 1, 4), half:half + quarter],
            held.at[x, wrap(y + 1, 4), half + quarter:rows],
        ]
        for lane, device in enumerate(self.targets(True)):
            self.arrive(0, lane, self.near(lane))
            self.go(1, lane, parts[lane], parts[lane], device)

    def spread(self):
        x, y, held, half, quarter, rows = self.x, self.y, self.held, self.half, self.quarter, self.rows
        far_x, far_y = wrap(x + 2, 4), wrap(y + 2, 4)
        for lane, part in enumerate([
            held.at[far_x, y, 0:quarter],
            held.at[far_x, y, quarter:half],
            held.at[x, far_y, half:half + quarter],
            held.at[x, far_y, half + quarter:rows],
        ]):
            self.arrive(1, lane, part)
        self.own.wait()
        line_x, line_y = held.at[:, y, 0:half], held.at[x, :, half:rows]
        for lane, device in enumerate(self.targets(False)):
            part = line_x if lane < 2 else line_y
            self.go(2, lane, part, part, device)

    def close(self):
        x, y, held, half, rows = self.x, self.y, self.held, self.half, self.rows
        whole = [
            held.at[:, wrap(y - 1, 4), 0:half],
            held.at[:, wrap(y + 1, 4), 0:half],
            held.at[wrap(x - 1, 4), :, half:rows],
            held.at[wrap(x + 1, 4), :, half:rows],
        ]
        parts = [
            held.at[0:2, wrap(y - 1, 4), 0:half],
            held.at[2:4, wrap(y + 1, 4), 0:half],
            held.at[wrap(x - 1, 4), 0:2, half:rows],
            held.at[wrap(x + 1, 4), 2:4, half:rows],
        ]
        for lane, device in enumerate(self.targets(False)):
            self.arrive(2, lane, whole[lane])
            self.go(3, lane, parts[lane], parts[lane], device)

    def finish(self):
        x, y, held, half, rows = self.x, self.y, self.held, self.half, self.rows
        far_x, far_y = wrap(x + 2, 4), wrap(y + 2, 4)
        for lane, part in enumerate([
            held.at[0:2, far_y, 0:half],
            held.at[2:4, far_y, 0:half],
            held.at[far_x, 0:2, half:rows],
            held.at[far_x, 2:4, half:rows],
        ]):
            self.arrive(3, lane, part)

    def block(self, start, width, tile):
        per_tile = 256 // width
        found = []
        for piece in range(per_tile):
            run = tile * per_tile + piece
            found.append(self.held[run // 4, run % 4, start:start + width])
        return found


class Ring:
    def __init__(self, source, held, send, recv, partner_send, partner_recv, local, at):
        self.source, self.held, self.send, self.recv = source, held, send, recv
        self.partner_send, self.partner_recv, self.local = partner_send, partner_recv, local
        self.r, self.z, self.core = at
        self.started = []

    def slot(self, z, core):
        return self.held.at[wrap(z, 8) * 2 + core, 0:256]

    def device(self, z, core):
        return (self.r, wrap(z, 8) * 2 + core)

    def go(self, step, lane, src, dst):
        shift = 1 if lane == 0 else -1
        copy = remote(src, dst, self.send.at[step, lane], self.recv.at[step, lane], self.device(self.z + shift, self.core))
        copy.start()
        self.started.append(copy)

    def share(self, index, src, dst):
        copy = remote(src, dst, self.partner_send.at[index], self.partner_recv.at[index], self.device(self.z, 1 - self.core))
        copy.start()
        self.started.append(copy)

    def arrive(self, step, lane, dst):
        remote(dst, dst, self.send.at[step, lane], self.recv.at[step, lane], self.device(self.z + 1, self.core)).wait_recv()

    def open(self):
        own = self.slot(self.z, self.core)
        for lane in range(2):
            self.go(0, lane, self.source, own)
        self.share(0, self.source, own)
        self.own = pltpu.make_async_copy(self.source, own, self.local)
        self.own.start()

    def step(self, number):
        for lane in range(2):
            distance = -number if lane == 0 else number
            tile = self.slot(self.z + distance, self.core)
            self.arrive(number - 1, lane, tile)
            if number < 3:
                self.go(number, lane, tile, tile)
            else:
                part = self.held.at[wrap(self.z + distance, 8) * 2 + self.core, 128 * lane:128 * lane + 128]
                self.go(number, lane, part, part)
            self.share(2 * number - 1 + lane, tile, tile)

    def finish(self):
        far = wrap(self.z + 4, 8) * 2 + self.core
        for lane in range(2):
            self.arrive(3, lane, self.held.at[far, 128 * lane:128 * lane + 128])
        tile = self.slot(self.z + 4, self.core)
        self.share(7, tile, tile)
        other = 1 - self.core
        for index, distance in enumerate([0, -1, 1, -2, 2, -3, 3, 4]):
            tile = self.slot(self.z + distance, other)
            remote(tile, tile, self.partner_send.at[index], self.partner_recv.at[index], self.device(self.z, other)).wait_recv()
        self.own.wait()


class Node:
    def __init__(self, held, rows, chips, send, recv, partner_send, partner_recv, at):
        self.held, self.rows, self.chips = held, rows, chips
        self.send, self.recv, self.partner_send, self.partner_recv = send, recv, partner_send, partner_recv
        self.r, self.z, self.core = at
        self.first = self.z - lax.rem(self.z, chips)
        self.place = lax.rem(self.z, chips)
        self.started = []

    def slot(self, place, core):
        return self.held.at[place * 2 + core, self.rows]

    def share(self, index, tile):
        copy = remote(tile, tile, self.partner_send.at[index], self.partner_recv.at[index],
                      (self.r, self.z * 2 + 1 - self.core))
        copy.start()
        self.started.append(copy)

    def open(self):
        tile = self.slot(self.place, self.core)
        for hop in range(1, self.chips):
            target = wrap(self.place + hop, self.chips)
            copy = remote(tile, tile, self.send.at[hop], self.recv.at[hop], (self.r, (self.first + target) * 2 + self.core))
            copy.start()
            self.started.append(copy)
        self.share(0, tile)

    def relay(self):
        for hop in range(1, self.chips):
            tile = self.slot(wrap(self.place - hop, self.chips), self.core)
            remote(tile, tile, self.send.at[hop], self.recv.at[hop], (self.r, self.z * 2 + 1 - self.core)).wait_recv()
            self.share(hop, tile)

    def finish(self):
        other = 1 - self.core
        for hop in range(self.chips):
            tile = self.slot(wrap(self.place - hop, self.chips), other)
            remote(tile, tile, self.partner_send.at[hop], self.partner_recv.at[hop], (self.r, self.z * 2 + other)).wait_recv()


class Chain:
    def __init__(self, held, rows, send, recv, partner_send, partner_recv, at):
        self.held, self.rows = held, rows
        self.send, self.recv, self.partner_send, self.partner_recv = send, recv, partner_send, partner_recv
        self.r, self.z, self.core = at
        self.first = self.z - lax.rem(self.z, 4)
        place = lax.rem(self.z, 4)
        upper, odd = lax.div(place, 2), lax.rem(place, 2)
        self.beside, self.across = place + 1 - 2 * odd, 3 - place
        self.inner = (upper + odd) == 1
        self.order = [place, self.beside, 2 - upper, 3 - 3 * upper]
        self.started, self.started_inner = [], []

    def slot(self, place, core):
        return self.held.at[place * 2 + core, self.rows]

    def copy(self, index, lane, place, target):
        tile = self.slot(place, self.core)
        return remote(tile, tile, self.send.at[index], self.recv.at[lane], (self.r, (self.first + target) * 2 + self.core))

    def share(self, index):
        tile = self.slot(self.order[index], self.core)
        copy = remote(tile, tile, self.partner_send.at[index], self.partner_recv.at[index],
                      (self.r, self.z * 2 + 1 - self.core))
        copy.start()
        self.started.append(copy)

    def inward(self, copy):
        self.started_inner.append(copy)

        @pl.when(self.inner)
        def _():
            copy.start()

    def open(self):
        self.inward(self.copy(1, 1, self.order[0], self.across))
        copy = self.copy(0, 0, self.order[0], self.beside)
        copy.start()
        self.started.append(copy)
        self.share(0)

    def relay(self):
        targets = [self.across, self.beside, self.beside]
        lanes = [2, 1, 2]
        for lane in range(3):
            tile = self.slot(self.order[lane + 1], self.core)
            remote(tile, tile, self.send.at[0], self.recv.at[lane], (self.r, self.z * 2 + 1 - self.core)).wait_recv()
            self.inward(self.copy(2 + lane, lanes[lane], self.order[lane + 1], targets[lane]))
            self.share(lane + 1)

    def finish(self):
        other = 1 - self.core
        for index in range(4):
            tile = self.slot(self.order[index], other)
            remote(tile, tile, self.partner_send.at[index], self.partner_recv.at[index], (self.r, self.z * 2 + other)).wait_recv()

    def drain(self):
        @pl.when(self.inner)
        def _():
            for copy in self.started_inner:
                copy.wait_send()


class Turn:
    def __init__(self, source, place, send, recv, partner_send, partner_recv, local, at):
        self.source, self.place = source, place
        self.send, self.recv, self.partner_send, self.partner_recv, self.local = send, recv, partner_send, partner_recv, local
        self.r, self.c, self.core = at
        self.started = []

    def open(self):
        self.own = pltpu.make_async_copy(self.source.at[self.r], self.place(self.r, self.core), self.local)
        self.own.start()
        for hop in range(1, 16):
            target = wrap(self.r + hop, 16)
            copy = remote(self.source.at[target], self.place(self.r, self.core), self.send.at[hop], self.recv.at[hop], (target, self.c))
            copy.start()
            self.started.append(copy)

    def share(self, hop):
        part = self.place(wrap(self.r - hop, 16), self.core)
        copy = remote(part, part, self.partner_send.at[hop], self.partner_recv.at[hop], (self.r, self.c + 1 - 2 * self.core))
        copy.start()
        self.started.append(copy)

    def relay(self):
        self.own.wait()
        self.share(0)
        for hop in range(1, 16):
            part = self.place(wrap(self.r - hop, 16), self.core)
            remote(part, part, self.send.at[hop], self.recv.at[hop], (wrap(self.r + 1, 16), self.c)).wait_recv()
            self.share(hop)

    def finish(self):
        for hop in range(16):
            part = self.place(wrap(self.r - hop, 16), 1 - self.core)
            remote(part, part, self.partner_send.at[hop], self.partner_recv.at[hop],
                   (self.r, self.c + 1 - 2 * self.core)).wait_recv()


def kernel(root_in, l_one_in, l_two_in, l_three_in, d_one_in, d_two_in, d_three_in, out_one, out_two, out_three,
           root, l_one, l_two, l_three, d_one, d_two, d_three, p_zero, p_one, p_two, p_three, g_one, g_two, g_three, turn_one, turn_two, turn_cross, sums, gained,
           plane_send, plane_recv, ring_send, ring_recv, ring_core_send, ring_core_recv,
           node_send, node_recv, node_core_send, node_core_recv,
           chain_send, chain_recv, chain_core_send, chain_core_recv, swap_send, swap_recv,
           turn_send, turn_recv, turn_core_send, turn_core_recv, last_send, last_recv, local, fetched):
    r, c = lax.axis_index("row"), lax.axis_index("col")
    x, y = lax.div(r, 4), lax.rem(r, 4)
    z, core = lax.div(c, 2), lax.rem(c, 2)
    eighth, quarter = lax.rem(c, 8), lax.rem(c, 4)

    fetches = [
        pltpu.make_async_copy(source, held, fetched.at[index])
        for index, (source, held) in enumerate([
            (l_one_in, l_one), (root_in, root), (l_two_in, l_two), (l_three_in, l_three),
            (d_one_in, d_one), (d_two_in, d_two), (d_three_in, d_three),
        ])
    ]
    for fetch in fetches:
        fetch.start()

    barrier = pltpu.get_barrier_semaphore()
    for hop in range(1, 16):
        pl.semaphore_signal(barrier, inc=1, device_id=(wrap(r + hop, 16), c), device_id_type=MESH)
    for hop in range(1, 8):
        pl.semaphore_signal(barrier, inc=1, device_id=(r, wrap(z + hop, 8) * 2 + core), device_id_type=MESH)
    pl.semaphore_signal(barrier, inc=1, device_id=(r, z * 2 + 1 - core), device_id_type=MESH)
    pl.semaphore_wait(barrier, 23)
    for fetch in fetches:
        fetch.wait()

    planes = [
        Plane(source, held, plane_send.at[level], plane_recv.at[level], local.at[level], (x, y, c))
        for level, (source, held) in enumerate([(l_one, g_one), (l_two, g_two), (l_three, g_three)])
    ]
    one, two, three = planes
    ring = Ring(root, p_zero, ring_send, ring_recv, ring_core_send, ring_core_recv, local.at[3], (r, z, core))

    def node(index, held, rows, chips):
        return Node(held, rows, chips, node_send.at[index], node_recv.at[index], node_core_send.at[index],
                    node_core_recv.at[index], (r, z, core))

    def chain(index, held, rows):
        return Chain(held, rows, chain_send.at[index], chain_recv.at[index], chain_core_send.at[index],
                     chain_core_recv.at[index], (r, z, core))

    s01 = [chain(0, p_one, slice(0, 256)), chain(1, p_one, slice(256, 512))]
    s11 = chain(2, p_one, slice(512, 768))
    s02 = node(0, p_two, slice(0, 512), 2)
    s12 = node(1, p_two, slice(512, 768), 2)
    s22 = node(2, p_two, slice(768, 896), 2)

    def turn(index, source, place):
        return Turn(source, place, turn_send.at[index], turn_recv.at[index], turn_core_send.at[index],
                    turn_core_recv.at[index], local.at[4 + index], (r, c, core))

    def rows_at(start, size, which):
        return pl.ds(pl.multiple_of(start + size * which, size), size)

    def half_turn(half):
        lanes = slice(128 * half, 128 * half + 128)
        return turn(2 + half, turn_one.at[half], lambda run, which: p_zero.at[run, rows_at(256, 128, which), lanes])

    t01 = [half_turn(0), half_turn(1)]
    t02 = turn(0, turn_two, lambda run, which: p_zero.at[run, rows_at(512, 64, which)])
    t12 = turn(1, turn_cross,
               lambda run, which: p_one.at[lax.div(run, 2), rows_at(768, 64, which),
                                           pl.ds(pl.multiple_of(lax.rem(run, 2) * 128, 128), 128)])

    def store(held, index, start, value):
        rows = value.shape[0]
        high, low = halves(value)
        held[index, start:start + rows] = high
        held[index, start + rows:start + 2 * rows] = low

    def zero_part(plane, first, last):
        return product([p_zero[k, first:last] for k in range(16)],
                       [piece for k in range(16) for piece in plane.block(0, 256, k)])

    def one_part(plane, first, last):
        return product([p_one[k, first:last] for k in range(8)],
                       [piece for k in range(8) for piece in plane.block(256, 128, k)])

    def two_part(plane, first, last):
        return product([p_two[k, first:last] for k in range(4)],
                       [piece for k in range(4) for piece in plane.block(384, 64, k)])

    one.open()
    ring.open()
    one.cross()
    ring.step(1)
    one.spread()
    two.open()
    ring.step(2)
    one.close()
    two.cross()
    three.open()
    ring.step(3)
    one.finish()
    two.spread()
    three.cross()
    ring.finish()

    for half in range(2):
        value = -zero_part(one, 128 * half, 128 * half + 128)
        store(p_one, eighth, 256 * half, value)
        s01[half].open()
        out_one[0, 128 * half:128 * half + 128] = value

    two.close()
    three.spread()
    for half in range(2):
        s01[half].relay()
        s01[half].finish()
        for k in range(8):
            tile = p_one[k, rows_at(256 * half, 128, core)]
            turned = tile.T
            turn_one[half, 2 * k] = turned[0:128]
            turn_one[half, 2 * k + 1] = turned[128:256]
        t01[half].open()

    two.finish()
    value = -(zero_part(two, 0, 256) + folded_halves(one_part(two, 0, 512)))
    store(p_two, quarter, 0, value)
    s02.open()
    out_two[0, 0:256] = value
    three.close()

    for half in range(2):
        t01[half].relay()
    for half in range(2):
        t01[half].finish()
    value = d_one[...].astype(F32) - folded(zero_part(one, 256, 512))
    store(p_one, eighth, 512, value)
    s11.open()
    out_one[0, 256:384] = value

    s02.relay()
    s02.finish()
    for k in range(4):
        tile = p_two[k, rows_at(0, 256, core)]
        turned = tile.T
        for piece in range(4):
            turn_two[4 * k + piece] = turned[64 * piece:64 * piece + 64]
    t02.open()

    early = zero_part(two, 256, 512)
    s11.relay()
    s11.finish()
    value = -folded(early + one_part(two, 512, 768))
    store(p_two, quarter, 512, value)
    s12.open()
    out_two[0, 256:384] = value

    three.finish()
    upper = -(zero_part(three, 0, 256) + folded_halves(one_part(three, 0, 512)) + folded(two_part(three, 0, 512)))
    out_three[0, 0:256] = upper
    high, low = halves(upper)
    p_three[core, 0:256] = high
    p_three[core, 384:640] = low
    early = zero_part(three, 256, 512) + one_part(three, 512, 768)
    s12.relay()
    s12.finish()
    for k in range(4):
        tile = p_two[k, rows_at(512, 128, core)]
        turned = tile.T
        for piece in range(4):
            turn_cross[4 * k + piece] = turned[64 * piece:64 * piece + 64]
    t12.open()

    middle = -folded(early + two_part(three, 512, 768))
    out_three[0, 256:384] = middle
    high, low = halves(middle)
    p_three[core, 256:384] = high
    p_three[core, 640:768] = low

    def swapped(index, rows):
        mine, theirs = p_three.at[core, rows], p_three.at[1 - core, rows]
        device = (r, z * 2 + 1 - core)
        return (remote(mine, mine, swap_send.at[index], swap_recv.at[index], device),
                remote(theirs, theirs, swap_send.at[index], swap_recv.at[index], device))

    def inner_terms(which, start, size, factor):
        turned = jnp.concatenate([p_three[which, start:start + size].T, p_three[which, start + size:start + 2 * size].T], 0)
        return folded(jnp.dot(turned, factor, preferred_element_type=F32))

    first_swap, first_gain = swapped(0, slice(0, 768))
    first_swap.start()

    t02.relay()
    t12.relay()
    t02.finish()
    early = zero_part(two, 512, 640)
    t12.finish()
    value = d_two[...].astype(F32) - folded(early + one_part(two, 768, 896))
    store(p_two, quarter, 768, value)
    s22.open()
    out_two[0, 384:448] = value
    first_gain.wait_recv()
    for which in range(2):
        partial = inner_terms(which, 0, 384, l_three[0:384])
        for piece in range(8):
            sums[8 * which + piece] = partial[32 * piece:32 * piece + 32]
    early = zero_part(three, 512, 640) + one_part(three, 768, 896)
    s22.relay()
    s22.finish()

    lower = -folded(early + two_part(three, 768, 896))
    high, low = halves(lower)
    p_three[core, 768:832] = high
    p_three[core, 832:896] = low
    last_swap, last_gain = swapped(1, slice(768, 896))
    last_swap.start()
    out_three[0, 384:448] = lower
    last_gain.wait_recv()
    for which in range(2):
        partial = inner_terms(which, 768, 64, l_three[384:448])
        for piece in range(8):
            sums[8 * which + piece] = sums[8 * which + piece] + partial[32 * piece:32 * piece + 32]
    final = []
    for hop in range(1, 16):
        target = wrap(r + hop, 16)
        copy = remote(sums.at[target], gained.at[r], last_send.at[hop], last_recv.at[hop], (target, c))
        copy.start()
        final.append(copy)
    total = sums[r]
    for hop in range(1, 16):
        source = wrap(r - hop, 16)
        part = gained.at[source]
        remote(part, part, last_send.at[hop], last_recv.at[hop], (wrap(r + 1, 16), c)).wait_recv()
        total = total + gained[source]
    out_three[0, 448:480] = d_three[...].astype(F32) - total

    first_swap.wait_send()
    last_swap.wait_send()
    for group in [one, two, three, ring, *s01, s11, s02, s12, s22, *t01, t02, t12]:
        for copy in group.started:
            copy.wait_send()
    for group in [*s01, s11]:
        group.drain()
    for copy in final:
        copy.wait_send()


def per_device(root_block, l_one, dinv_one, l_two, dinv_two, l_three, dinv_three):
    vmem = pl.BlockSpec(memory_space=pltpu.VMEM)
    dma = pltpu.SemaphoreType.DMA
    return pl.pallas_call(
        kernel,
        out_shape=(
            pltpu.VMEM((1, 384, 256), F32),
            pltpu.VMEM((1, 448, 256), F32),
            pltpu.VMEM((1, 480, 256), F32),
        ),
        in_specs=[pl.BlockSpec(memory_space=pl.ANY)] * 7,
        out_specs=(vmem, vmem, vmem),
        scratch_shapes=[
            pltpu.VMEM((256, 256), BF16),
            pltpu.VMEM((256, 256), BF16),
            pltpu.VMEM((384, 256), BF16),
            pltpu.VMEM((448, 256), BF16),
            pltpu.VMEM((128, 256), BF16),
            pltpu.VMEM((64, 256), BF16),
            pltpu.VMEM((32, 256), BF16),
            pltpu.VMEM((16, 640, 256), BF16),
            pltpu.VMEM((8, 896, 256), BF16),
            pltpu.VMEM((4, 896, 256), BF16),
            pltpu.VMEM((2, 896, 256), BF16),
            pltpu.VMEM((4, 4, 256, 256), BF16),
            pltpu.VMEM((4, 4, 384, 256), BF16),
            pltpu.VMEM((4, 4, 448, 256), BF16),
            pltpu.VMEM((2, 16, 128, 128), BF16),
            pltpu.VMEM((16, 64, 256), BF16),
            pltpu.VMEM((16, 64, 128), BF16),
            pltpu.VMEM((16, 32, 256), F32),
            pltpu.VMEM((16, 32, 256), F32),
            dma((3, 4, 4)), dma((3, 4, 4)),
            dma((4, 2)), dma((4, 2)), dma((8,)), dma((8,)),
            dma((3, 2)), dma((3, 2)), dma((3, 2)), dma((3, 2)),
            dma((3, 5)), dma((3, 3)), dma((3, 4)), dma((3, 4)), dma((2,)), dma((2,)),
            dma((4, 16)), dma((4, 16)), dma((4, 16)), dma((4, 16)),
            dma((16,)), dma((16,)),
            dma((8,)), dma((7,)),
        ],
        compiler_params=pltpu.CompilerParams(
            collective_id=0, has_side_effects=True, vmem_limit_bytes=60 * 1024 * 1024
        ),
    )(root_block[0], l_one[0], l_two[0], l_three[0], dinv_one[0], dinv_two[0], dinv_three[0])


def solution(mesh):
    placed = (P("row", None, "col"),) * 7
    return jax.shard_map(
        per_device,
        mesh=mesh,
        in_specs=placed,
        out_specs=(P("row", None, "col"), P("row", None, "col"), P("row", None, "col")),
        check_vma=False,
    )
```
